32 devices in a mesh: kstr: 4 (over y, x), pw: 8 (over z, core).
Axes of the slice: x: 2, y: 2, z: 4, core: 2. Of those that a mesh axis runs over, the one named last changes fastest.
Arguments:
- states_re: bfloat16 [4, 256, 16384], P('kstr', None, 'pw'), may hold values from -8 to 8
- states_im: bfloat16 [4, 256, 16384], P('kstr', None, 'pw'), may hold values from -8 to 8
- gmap: int32 [16384], P('pw'), may hold values from 0 to 16383, as said below
Outputs:
- new_re: bfloat16 [4, 256, 16384], P('kstr', None, 'pw')
- new_im: bfloat16 [4, 256, 16384], P('kstr', None, 'pw')
The draws below stay inside these ranges and needn't reach their ends.
Inputs may be any that keep to these rules, and one draw needn't show every extreme that they name: gmap[G] = (G + o) mod 16384 for one offset o with 1 <= o < 16384.
All inputs are finite; a program needn't handle non-finite values.
Results may differ from the reference program's by a relative error of at most 0.008.
Values may be sent and summed in bfloat16 or wider, within the bound.
A program may use at most 64 MiB of HBM per device.

```python
import jax
import jax.numpy as jnp
from jax import lax

NB = 256
NPW = 16384
NEWTON = 4
STEPS = 2
NK = 4


def state_parts(key):
    base_key = jax.random.fold_in(key, 7)
    noise_key = jax.random.fold_in(key, 8)
    kpos = jnp.arange(NK, dtype=jnp.float32) / max(NK - 1, 1)
    base = jax.random.normal(base_key, (2, 1, NB, NPW), jnp.float32) * 0.7071
    noise = jax.random.normal(noise_key, (2, NK, NB, NPW), jnp.float32) * 0.7071
    bands = jnp.ones((1, 1, NB, 1), jnp.float32)
    amplitude = 1.0 / (1.0 + 2.0 * kpos)
    level = (0.15 * (1.0 + 2.0 * kpos))[None, :, None, None]
    gpos = jnp.arange(NPW, dtype=jnp.float32) / NPW
    column = (0.6 + 0.8 * gpos)[None, None, None, :]
    field = jnp.clip(amplitude[None, :, None, None] * (base + level * column * bands * noise), -8.0, 8.0)
    return (field[0], field[1])


def draw_states_re(key, part):
    return state_parts(key)[0].astype(jnp.bfloat16)


def draw_states_im(key, part):
    return state_parts(key)[1].astype(jnp.bfloat16)


def draw_gmap(key, part):
    offset = jax.random.randint(jax.random.fold_in(key, 11), (), 1, NPW)
    index = jnp.arange(NPW, dtype=jnp.int32)
    return jnp.mod(index + offset, NPW).astype(jnp.int32)


def setup_inputs(seed: int = 0) -> dict:
    key_list = jax.random.split(jax.random.key(seed), 4)
    states_re = draw_states_re(jax.random.fold_in(key_list[3], 71), 0)
    states_im = draw_states_im(jax.random.fold_in(key_list[3], 71), 0)
    gmap = draw_gmap(jax.random.fold_in(key_list[3], 71), 0)
    return {"states_re": states_re, "states_im": states_im, "gmap": gmap}


HIGH = lax.Precision.HIGHEST
EPS_SCALE = 1e-06
EPS_NORM = 1e-06
TAU_STEP = 0.25

def complex_mul(a_re, a_im, b_re, b_im):

    def matmul(left, right):
        return jnp.einsum('kij,kjl->kil', left, right, precision=HIGH)
    return (matmul(a_re, b_re) - matmul(a_im, b_im), matmul(a_re, b_im) + matmul(a_im, b_re))

def invert(s_re, s_im):
    magnitude = jnp.sqrt(s_re * s_re + s_im * s_im)
    colmax = lax.optimization_barrier(jnp.max(lax.optimization_barrier(jnp.sum(magnitude, axis=1)), axis=1))
    rowmax = lax.optimization_barrier(jnp.max(lax.optimization_barrier(jnp.sum(magnitude, axis=2)), axis=1))
    factor = (1.0 / (colmax * rowmax + EPS_SCALE))[:, None, None]
    x_re = jnp.swapaxes(s_re, 1, 2) * factor
    x_im = -jnp.swapaxes(s_im, 1, 2) * factor
    for turn in range(NEWTON):
        p_re, p_im = complex_mul(s_re, s_im, x_re, x_im)
        q_re, q_im = complex_mul(x_re, x_im, p_re, p_im)
        x_re = 2.0 * x_re - q_re
        x_im = 2.0 * x_im - q_im
    return (x_re, x_im)

def product(form, left, right):
    return jnp.einsum(form, left.astype(jnp.float32), right.astype(jnp.float32), precision=HIGH)

def reference(states_re, states_im, gmap):
    field_re, field_im = (states_re, states_im)
    for step in range(STEPS):
        next_re = jnp.concatenate([field_re[1:], field_re[:1][:, :, gmap]], 0)
        next_im = jnp.concatenate([field_im[1:], field_im[:1][:, :, gmap]], 0)
        s_re = (product('kmg,kng->kmn', field_re, next_re) + product('kmg,kng->kmn', field_im, next_im)) / NPW
        s_im = (product('kmg,kng->kmn', field_re, next_im) - product('kmg,kng->kmn', field_im, next_re)) / NPW
        x_re, x_im = invert(s_re, s_im)
        xb_re = x_re.astype(jnp.bfloat16)
        xb_im = x_im.astype(jnp.bfloat16)
        a_re = product('kmn,kmg->kng', xb_re, next_re) - product('kmn,kmg->kng', xb_im, next_im)
        a_im = product('kmn,kmg->kng', xb_re, next_im) + product('kmn,kmg->kng', xb_im, next_re)
        c_re = (product('kmn,kmg->kng', xb_re, field_re) + product('kmn,kmg->kng', xb_im, field_im)).astype(jnp.bfloat16)
        c_im = (product('kmn,kmg->kng', xb_re, field_im) - product('kmn,kmg->kng', xb_im, field_re)).astype(jnp.bfloat16)
        head_re = jnp.zeros_like(c_re[-1]).at[:, gmap].set(c_re[-1])
        head_im = jnp.zeros_like(c_im[-1]).at[:, gmap].set(c_im[-1])
        d_re = jnp.concatenate([head_re[None], c_re[:-1]], 0).astype(jnp.float32)
        d_im = jnp.concatenate([head_im[None], c_im[:-1]], 0).astype(jnp.float32)
        g_re = a_im - d_im
        g_im = d_re - a_re
        total = jnp.sum(g_re * g_re + g_im * g_im)
        rms = jnp.sqrt(total / (2 * NK * NB * NPW) + EPS_NORM)
        field_re = (field_re.astype(jnp.float32) + TAU_STEP * g_re / rms).astype(jnp.bfloat16)
        field_im = (field_im.astype(jnp.float32) + TAU_STEP * g_im / rms).astype(jnp.bfloat16)
    return (field_re, field_im)
```

```python
import jax
import jax.numpy as jnp
from jax import lax
from jax.experimental import pallas as pl
from jax.experimental.pallas import tpu as pltpu
from jax.sharding import PartitionSpec as P

NEWTON = 4
STEPS = 2


HIGH = lax.Precision.HIGHEST
EPS_SCALE = 1e-06
EPS_NORM = 1e-06
TAU_STEP = 0.25


def shifted(value, axis, by):
    count = lax.axis_size(axis)
    return lax.ppermute(value, axis, [(i, (i + by) % count) for i in range(count)])


def padded_2(block, sides, width):
    for axis, dim in sides:
        count = lax.axis_size(axis)
        forward = [(i, i + 1) for i in range(count - 1)]
        forward.append((count - 1, 0))
        backward = [(target, source) for source, target in forward]
        low = lax.ppermute(
            lax.slice_in_dim(block, block.shape[dim] - width, None, axis=dim), axis, forward
        )
        high = lax.ppermute(lax.slice_in_dim(block, 0, width, axis=dim), axis, backward)
        block = jnp.concatenate([low, block, high], axis=dim)
    return block


def complex_mul(left, right):

    def matmul(first, second):
        return jnp.einsum("kij,kjl->kil", first, second, precision=HIGH)

    real = matmul(left[:, 0], right[:, 0]) - matmul(left[:, 1], right[:, 1])
    imag = matmul(left[:, 0], right[:, 1]) + matmul(left[:, 1], right[:, 0])
    return jnp.stack([real, imag], 1)


def start_inverse(whole):
    magnitude = jnp.sqrt(whole[:, 0] * whole[:, 0] + whole[:, 1] * whole[:, 1])
    colmax = jnp.max(jnp.sum(magnitude, axis=1), axis=1)
    rowmax = jnp.max(jnp.sum(magnitude, axis=2), axis=1)
    factor = (1.0 / (colmax * rowmax + EPS_SCALE))[:, None, None]
    return jnp.stack(
        [jnp.swapaxes(whole[:, 0], 1, 2) * factor, -jnp.swapaxes(whole[:, 1], 1, 2) * factor], 1
    )


def newton_full(whole):
    iterate = start_inverse(whole)
    for turn in range(NEWTON):
        iterate = 2.0 * iterate - complex_mul(iterate, complex_mul(whole, iterate))
    return iterate


def bf_product(form, left, right):
    return jnp.einsum(form, left, right, preferred_element_type=jnp.float32)


def dual_terms(rounded, states):
    real = bf_product("kmn,kmg->kng", rounded[:, 0], states[:, 0]) + bf_product(
        "kmn,kmg->kng", rounded[:, 1], states[:, 1]
    )
    imag = bf_product("kmn,kmg->kng", rounded[:, 0], states[:, 1]) - bf_product(
        "kmn,kmg->kng", rounded[:, 1], states[:, 0]
    )
    return jnp.stack([real, imag], 1).astype(jnp.bfloat16)


def rotate_columns(block, amount, width):
    blocks_off = amount // width
    rest = amount % width
    plane_size = lax.axis_size("pw")
    for bit in range((plane_size - 1).bit_length()):
        moved = shifted(block, "pw", -(1 << bit))
        block = jnp.where(jnp.bitwise_and(jnp.right_shift(blocks_off, bit), 1) == 1, moved, block)
    after = shifted(block, "pw", -1)
    joined = jnp.concatenate([block, after], block.ndim - 1)
    return lax.dynamic_slice_in_dim(joined, rest, width, block.ndim - 1)


def general_body(states_re, states_im, gmap):
    kpoints, bands, width = states_re.shape
    string_size = lax.axis_size("kstr")
    plane_size = lax.axis_size("pw")
    string_index = lax.axis_index("kstr")
    total_width = width * plane_size
    offset = jnp.mod(gmap[0] - lax.axis_index("pw") * width, total_width)
    back_offset = jnp.mod(total_width - offset, total_width)
    at_first = string_index == 0
    at_last = string_index == string_size - 1
    count_all = 2 * kpoints * string_size * bands * width * plane_size
    states = jnp.stack([states_re, states_im], 1)
    for step in range(STEPS):
        padded = padded_2(states, (("kstr", 0),), 1)
        ahead = padded[-1:]
        behind = padded[:1]
        turned = rotate_columns(ahead, offset, width)
        ahead = jnp.where(at_last, turned, ahead)
        following = jnp.concatenate([states[1:], ahead], 0)
        s_re = bf_product("kmg,kng->kmn", states[:, 0], following[:, 0]) + bf_product(
            "kmg,kng->kmn", states[:, 1], following[:, 1]
        )
        s_im = bf_product("kmg,kng->kmn", states[:, 0], following[:, 1]) - bf_product(
            "kmg,kng->kmn", states[:, 1], following[:, 0]
        )
        partial_value = jnp.stack([s_re, s_im], 1)
        whole = lax.psum(partial_value, "pw") / (width * plane_size)
        inverse = newton_full(whole)
        rounded = inverse.astype(jnp.bfloat16)
        a_re = bf_product("kmn,kmg->kng", rounded[:, 0], following[:, 0]) - bf_product(
            "kmn,kmg->kng", rounded[:, 1], following[:, 1]
        )
        a_im = bf_product("kmn,kmg->kng", rounded[:, 0], following[:, 1]) + bf_product(
            "kmn,kmg->kng", rounded[:, 1], following[:, 0]
        )
        earlier = dual_terms(rounded[:-1], states[:-1])
        previous_inverse = shifted(rounded, "kstr", 1)
        arrived = dual_terms(previous_inverse, behind)
        placed = rotate_columns(arrived, back_offset, width)
        arrived = jnp.where(at_first, placed, arrived)
        incoming = jnp.concatenate([arrived, earlier], 0).astype(jnp.float32)
        g_re = a_im - incoming[:, 1]
        g_im = incoming[:, 0] - a_re
        total = lax.psum(jnp.sum(g_re * g_re + g_im * g_im), ("kstr", "pw"))
        rms = jnp.sqrt(total / count_all + EPS_NORM)
        new_re = (states[:, 0].astype(jnp.float32) + TAU_STEP * g_re / rms).astype(jnp.bfloat16)
        new_im = (states[:, 1].astype(jnp.float32) + TAU_STEP * g_im / rms).astype(jnp.bfloat16)
        states = jnp.stack([new_re, new_im], 1)
    return (states[:, 0], states[:, 1])


def rank_of(k, p, planes):
    return k * planes + p


def exchange(name, ident, peers, here, there, copies, args, outs, parts=1):
    n_in = len(args)

    def kernel(*refs):
        data, (send, recv, local) = refs[:-3], refs[-3:]
        barrier = pltpu.get_barrier_semaphore()

        def greet(step, carry):
            pl.semaphore_signal(
                barrier, inc=1, device_id=there(step), device_id_type=pl.DeviceIdType.MESH
            )
            return carry

        lax.fori_loop(1, peers, greet, 0)
        pl.semaphore_wait(barrier, peers - 1)

        def remote(step):
            target = there(step)
            return [
                pltpu.make_async_remote_copy(
                    src_ref=source,
                    dst_ref=place,
                    send_sem=send.at[step, index],
                    recv_sem=recv.at[step, index],
                    device_id=target,
                    device_id_type=pl.DeviceIdType.MESH,
                )
                for index, (source, place) in enumerate(copies(data, target))
            ]

        def begin(step, carry):
            for copy in remote(step):
                copy.start()
            return carry

        def finish(step, carry):
            for copy in remote(step):
                copy.wait()
            return carry

        lax.fori_loop(1, peers, begin, 0)
        own = [
            pltpu.make_async_copy(source, place, local.at[index])
            for index, (source, place) in enumerate(copies(data, here()))
        ]
        for copy in own:
            copy.start()
        for copy in own:
            copy.wait()
        lax.fori_loop(1, peers, finish, 0)

    return pl.pallas_call(
        kernel,
        out_shape=outs,
        in_specs=[pl.BlockSpec(memory_space=pltpu.VMEM)] * n_in,
        out_specs=jax.tree.map(lambda _: pl.BlockSpec(memory_space=pltpu.VMEM), outs),
        scratch_shapes=[
            pltpu.SemaphoreType.DMA((peers, parts)),
            pltpu.SemaphoreType.DMA((peers, parts)),
            pltpu.SemaphoreType.DMA((parts,)),
        ],
        compiler_params=pltpu.CompilerParams(collective_id=ident, has_side_effects=True),
        name=name,
    )(*args)


def spread_body(strings, planes, states_re, states_im, gmap):
    _, bands, width = states_re.shape
    count = strings * planes
    piece = width // strings
    total_width = width * planes
    rows = 2 * bands // count
    half = count // 2
    share = bands // planes
    count_all = 2 * strings * bands * total_width
    bf16, f32 = jnp.bfloat16, jnp.float32

    def place():
        return lax.axis_index("kstr"), lax.axis_index("pw")

    def over_string(step):
        k, p = place()
        return (lax.rem(k + step, strings), p)

    def over_planes(step):
        k, p = place()
        return (k, lax.rem(p + step, planes))

    def over_all(step):
        k, p = place()
        peer = lax.rem(rank_of(k, p, planes) + step, count)
        return (peer // planes, lax.rem(peer, planes))

    def columns(index, size):
        return pl.ds(pl.multiple_of(index * size, size), size)

    def band_rows(rank):
        return pl.ds(pl.multiple_of(lax.rem(rank, half) * rows, rows), rows)

    def spread(refs, target):
        re, im, out = refs
        k, _ = place()
        cut = columns(target[0], piece)
        return [(re.at[:, cut], out.at[k, 0]), (im.at[:, cut], out.at[k, 1])]

    def collect(refs, target):
        new, re, im = refs
        k, _ = place()
        cut = columns(k, piece)
        return [(new.at[target[0], 0], re.at[:, cut]), (new.at[target[0], 1], im.at[:, cut])]

    def to_bands(refs, target):
        own, out = refs
        k, p = place()
        rank = rank_of(target[0], target[1], planes)
        which = (rank // half) * (strings - 1)
        return [(own.at[which, :, band_rows(rank), :], out.at[:, :, columns(p * strings + k, piece)])]

    def from_bands(refs, target):
        rolled, out = refs
        rank = rank_of(*place(), planes)
        block = target[1] * strings + target[0]
        return [(rolled.at[:, :, columns(block, piece)], out.at[rank // half, :, band_rows(rank), :])]

    def sum_string(refs, target):
        part, out = refs
        return [(part.at[target[0]], out.at[place()[0]])]

    def sum_planes(refs, target):
        part, out = refs
        return [(part.at[:, columns(target[1], share), :], out.at[place()[1]])]

    def gather_planes(refs, target):
        part, out = refs
        return [(part, out.at[:, columns(place()[1], share), :])]

    def gather_string(refs, target):
        part, out = refs
        return [(part, out.at[place()[0]])]

    def gather_all(refs, target):
        part, out = refs
        return [(part, out.at[rank_of(*place(), planes)])]

    here = place
    offset = jnp.mod(gmap[0] - lax.axis_index("pw") * width, total_width)
    back_offset = jnp.mod(total_width - offset, total_width)
    amount = jnp.where(rank_of(*place(), planes) < half, offset, back_offset)

    shape = jax.ShapeDtypeStruct
    states = exchange(
        "spread", 1, strings, here, over_string, spread,
        (states_re[0], states_im[0]), shape((strings, 2, bands, piece), bf16), 2,
    )
    for step in range(STEPS):
        banded = exchange(
            "to_bands", 2, count, here, over_all, to_bands,
            (states,), shape((2, rows, total_width), bf16),
        )
        rolled = lax.dynamic_slice_in_dim(
            jnp.concatenate([banded, banded], 2), amount, total_width, 2
        )
        turned = exchange(
            "from_bands", 3, count, here, over_all, from_bands,
            (rolled,), shape((2, 2, bands, piece), bf16),
        )
        following = jnp.concatenate([states[1:], turned[:1]], 0)
        before = jnp.concatenate([turned[1:], states[:-1]], 0)
        s_re = bf_product("kmg,kng->kmn", states[:, 0], following[:, 0]) + bf_product(
            "kmg,kng->kmn", states[:, 1], following[:, 1]
        )
        s_im = bf_product("kmg,kng->kmn", states[:, 0], following[:, 1]) - bf_product(
            "kmg,kng->kmn", states[:, 1], following[:, 0]
        )
        partial_value = (jnp.stack([s_re, s_im], 1) / total_width).astype(bf16)
        pieces = exchange(
            "sum_string", 4, strings, here, over_string, sum_string,
            (partial_value,), shape((strings, 2, bands, bands), bf16),
        )
        part = jnp.sum(pieces.astype(f32), 0).astype(bf16)
        pieces = exchange(
            "sum_planes", 5, planes, here, over_planes, sum_planes,
            (part,), shape((planes, 2, share, bands), bf16),
        )
        part = jnp.sum(pieces.astype(f32), 0)
        whole = exchange(
            "gather_planes", 6, planes, here, over_planes, gather_planes,
            (part,), shape((2, bands, bands), f32),
        )
        rounded = newton_full(whole[None])[0].astype(bf16)
        inverse = exchange(
            "gather_string", 7, strings, here, over_string, gather_string,
            (rounded,), shape((strings, 2, bands, bands), bf16),
        )
        earlier = jnp.concatenate([inverse[-1:], inverse[:-1]], 0)
        a_re = bf_product("kmn,kmg->kng", inverse[:, 0], following[:, 0]) - bf_product(
            "kmn,kmg->kng", inverse[:, 1], following[:, 1]
        )
        a_im = bf_product("kmn,kmg->kng", inverse[:, 0], following[:, 1]) + bf_product(
            "kmn,kmg->kng", inverse[:, 1], following[:, 0]
        )
        incoming = dual_terms(earlier, before).astype(f32)
        g_re = a_im - incoming[:, 1]
        g_im = incoming[:, 0] - a_re
        local = jnp.sum(g_re * g_re + g_im * g_im)
        sums = exchange(
            "gather_all", 8, count, here, over_all, gather_all,
            (jnp.broadcast_to(local, (8, 128)),), shape((count, 8, 128), f32),
        )
        total = jnp.sum(sums[:, 0, 0])
        rms = jnp.sqrt(total / count_all + EPS_NORM)
        new_re = (states[:, 0].astype(f32) + TAU_STEP * g_re / rms).astype(bf16)
        new_im = (states[:, 1].astype(f32) + TAU_STEP * g_im / rms).astype(bf16)
        states = jnp.stack([new_re, new_im], 1)
    new_re, new_im = exchange(
        "collect", 9, strings, here, over_string, collect,
        (states,), (shape((bands, width), bf16), shape((bands, width), bf16)), 2,
    )
    return (new_re[None], new_im[None])


def solution(mesh):
    placed = (P("kstr", None, "pw"), P("kstr", None, "pw"), P("pw"))
    strings, planes = mesh.shape["kstr"], mesh.shape["pw"]

    def body(states_re, states_im, gmap):
        kpoints, bands, width = states_re.shape
        count = strings * planes
        fits = (
            kpoints == 1
            and strings > 1
            and planes > 1
            and width % (strings * 128) == 0
            and bands % (planes * 16) == 0
            and (2 * bands) % (count * 16) == 0
        )
        if not fits:
            return general_body(states_re, states_im, gmap)
        return spread_body(strings, planes, states_re, states_im, gmap)

    return jax.shard_map(
        body,
        mesh=mesh,
        in_specs=placed,
        out_specs=(P("kstr", None, "pw"), P("kstr", None, "pw")),
        check_vma=False,
    )
```

```python
import jax
import jax.numpy as jnp
from jax import lax
from jax.experimental import pallas as pl
from jax.experimental.pallas import tpu as pltpu
from jax.sharding import PartitionSpec as P

NEWTON = 4
STEPS = 2


HIGH = lax.Precision.HIGHEST
EPS_SCALE = 1e-06
EPS_NORM = 1e-06
TAU_STEP = 0.25


def shifted(value, axis, by):
    count = lax.axis_size(axis)
    return lax.ppermute(value, axis, [(i, (i + by) % count) for i in range(count)])


def padded_2(block, sides, width):
    for axis, dim in sides:
        count = lax.axis_size(axis)
        forward = [(i, i + 1) for i in range(count - 1)]
        forward.append((count - 1, 0))
        backward = [(target, source) for source, target in forward]
        low = lax.ppermute(
            lax.slice_in_dim(block, block.shape[dim] - width, None, axis=dim), axis, forward
        )
        high = lax.ppermute(lax.slice_in_dim(block, 0, width, axis=dim), axis, backward)
        block = jnp.concatenate([low, block, high], axis=dim)
    return block


def complex_mul(left, right):

    def matmul(first, second):
        return jnp.einsum("kij,kjl->kil", first, second, precision=HIGH)

    real = matmul(left[:, 0], right[:, 0]) - matmul(left[:, 1], right[:, 1])
    imag = matmul(left[:, 0], right[:, 1]) + matmul(left[:, 1], right[:, 0])
    return jnp.stack([real, imag], 1)


def start_inverse(whole):
    magnitude = jnp.sqrt(whole[:, 0] * whole[:, 0] + whole[:, 1] * whole[:, 1])
    colmax = jnp.max(jnp.sum(magnitude, axis=1), axis=1)
    rowmax = jnp.max(jnp.sum(magnitude, axis=2), axis=1)
    factor = (1.0 / (colmax * rowmax + EPS_SCALE))[:, None, None]
    return jnp.stack(
        [jnp.swapaxes(whole[:, 0], 1, 2) * factor, -jnp.swapaxes(whole[:, 1], 1, 2) * factor], 1
    )


def newton_full(whole):
    iterate = start_inverse(whole)
    for turn in range(NEWTON):
        iterate = 2.0 * iterate - complex_mul(iterate, complex_mul(whole, iterate))
    return iterate


def bf_product(form, left, right):
    return jnp.einsum(form, left, right, preferred_element_type=jnp.float32)


def dual_terms(rounded, states):
    real = bf_product("kmn,kmg->kng", rounded[:, 0], states[:, 0]) + bf_product(
        "kmn,kmg->kng", rounded[:, 1], states[:, 1]
    )
    imag = bf_product("kmn,kmg->kng", rounded[:, 0], states[:, 1]) - bf_product(
        "kmn,kmg->kng", rounded[:, 1], states[:, 0]
    )
    return jnp.stack([real, imag], 1).astype(jnp.bfloat16)


def rotate_columns(block, amount, width):
    blocks_off = amount // width
    rest = amount % width
    plane_size = lax.axis_size("pw")
    for bit in range((plane_size - 1).bit_length()):
        moved = shifted(block, "pw", -(1 << bit))
        block = jnp.where(jnp.bitwise_and(jnp.right_shift(blocks_off, bit), 1) == 1, moved, block)
    after = shifted(block, "pw", -1)
    joined = jnp.concatenate([block, after], block.ndim - 1)
    return lax.dynamic_slice_in_dim(joined, rest, width, block.ndim - 1)


def general_body(states_re, states_im, gmap):
    kpoints, bands, width = states_re.shape
    string_size = lax.axis_size("kstr")
    plane_size = lax.axis_size("pw")
    string_index = lax.axis_index("kstr")
    total_width = width * plane_size
    offset = jnp.mod(gmap[0] - lax.axis_index("pw") * width, total_width)
    back_offset = jnp.mod(total_width - offset, total_width)
    at_first = string_index == 0
    at_last = string_index == string_size - 1
    count_all = 2 * kpoints * string_size * bands * width * plane_size
    states = jnp.stack([states_re, states_im], 1)
    for step in range(STEPS):
        padded = padded_2(states, (("kstr", 0),), 1)
        ahead = padded[-1:]
        behind = padded[:1]
        turned = rotate_columns(ahead, offset, width)
        ahead = jnp.where(at_last, turned, ahead)
        following = jnp.concatenate([states[1:], ahead], 0)
        s_re = bf_product("kmg,kng->kmn", states[:, 0], following[:, 0]) + bf_product(
            "kmg,kng->kmn", states[:, 1], following[:, 1]
        )
        s_im = bf_product("kmg,kng->kmn", states[:, 0], following[:, 1]) - bf_product(
            "kmg,kng->kmn", states[:, 1], following[:, 0]
        )
        partial_value = jnp.stack([s_re, s_im], 1)
        whole = lax.psum(partial_value, "pw") / (width * plane_size)
        inverse = newton_full(whole)
        rounded = inverse.astype(jnp.bfloat16)
        a_re = bf_product("kmn,kmg->kng", rounded[:, 0], following[:, 0]) - bf_product(
            "kmn,kmg->kng", rounded[:, 1], following[:, 1]
        )
        a_im = bf_product("kmn,kmg->kng", rounded[:, 0], following[:, 1]) + bf_product(
            "kmn,kmg->kng", rounded[:, 1], following[:, 0]
        )
        earlier = dual_terms(rounded[:-1], states[:-1])
        previous_inverse = shifted(rounded, "kstr", 1)
        arrived = dual_terms(previous_inverse, behind)
        placed = rotate_columns(arrived, back_offset, width)
        arrived = jnp.where(at_first, placed, arrived)
        incoming = jnp.concatenate([arrived, earlier], 0).astype(jnp.float32)
        g_re = a_im - incoming[:, 1]
        g_im = incoming[:, 0] - a_re
        total = lax.psum(jnp.sum(g_re * g_re + g_im * g_im), ("kstr", "pw"))
        rms = jnp.sqrt(total / count_all + EPS_NORM)
        new_re = (states[:, 0].astype(jnp.float32) + TAU_STEP * g_re / rms).astype(jnp.bfloat16)
        new_im = (states[:, 1].astype(jnp.float32) + TAU_STEP * g_im / rms).astype(jnp.bfloat16)
        states = jnp.stack([new_re, new_im], 1)
    return (states[:, 0], states[:, 1])


def rank_of(k, p, planes):
    return k * planes + p


def exchange(name, ident, peers, here, there, copies, args, outs, parts=1):
    n_in = len(args)

    def kernel(*refs):
        data, (send, recv, local) = refs[:-3], refs[-3:]
        barrier = pltpu.get_barrier_semaphore()

        def greet(step, carry):
            pl.semaphore_signal(
                barrier, inc=1, device_id=there(step), device_id_type=pl.DeviceIdType.MESH
            )
            return carry

        lax.fori_loop(1, peers, greet, 0)
        pl.semaphore_wait(barrier, peers - 1)

        def remote(step):
            target = there(step)
            return [
                pltpu.make_async_remote_copy(
                    src_ref=source,
                    dst_ref=place,
                    send_sem=send.at[step, index],
                    recv_sem=recv.at[step, index],
                    device_id=target,
                    device_id_type=pl.DeviceIdType.MESH,
                )
                for index, (source, place) in enumerate(copies(data, target))
            ]

        def begin(step, carry):
            for copy in remote(step):
                copy.start()
            return carry

        def finish(step, carry):
            for copy in remote(step):
                copy.wait()
            return carry

        lax.fori_loop(1, peers, begin, 0)
        own = [
            pltpu.make_async_copy(source, place, local.at[index])
            for index, (source, place) in enumerate(copies(data, here()))
        ]
        for copy in own:
            copy.start()
        for copy in own:
            copy.wait()
        lax.fori_loop(1, peers, finish, 0)

    return pl.pallas_call(
        kernel,
        out_shape=outs,
        in_specs=[pl.BlockSpec(memory_space=pltpu.VMEM)] * n_in,
        out_specs=jax.tree.map(lambda _: pl.BlockSpec(memory_space=pltpu.VMEM), outs),
        scratch_shapes=[
            pltpu.SemaphoreType.DMA((peers, parts)),
            pltpu.SemaphoreType.DMA((peers, parts)),
            pltpu.SemaphoreType.DMA((parts,)),
        ],
        compiler_params=pltpu.CompilerParams(collective_id=ident, has_side_effects=True),
        name=name,
    )(*args)


def sum_everywhere(ident, strings, planes, local):
    def kernel(local_ref, out_ref, first, second, stage, send, recv):
        k, p = lax.axis_index("kstr"), lax.axis_index("pw")

        def string_peer(step):
            return (lax.rem(k + step, strings), p)

        def plane_peer(step):
            return (k, lax.rem(p + step, planes))

        barrier = pltpu.get_barrier_semaphore()
        peers = [string_peer(step) for step in range(1, strings)]
        peers += [plane_peer(step) for step in range(1, planes)]
        for peer in peers:
            pl.semaphore_signal(
                barrier, inc=1, device_id=peer, device_id_type=pl.DeviceIdType.MESH
            )
        pl.semaphore_wait(barrier, len(peers))

        def copy(source, place, slot):
            return pltpu.make_async_remote_copy(
                src_ref=source,
                dst_ref=place,
                send_sem=send.at[slot],
                recv_sem=recv.at[slot],
                device_id=peers[slot],
                device_id_type=pl.DeviceIdType.MESH,
            )

        copies = [copy(local_ref, first.at[k], slot) for slot in range(strings - 1)]
        for item in copies:
            item.start()
        first[k] = local_ref[...]
        for item in copies:
            item.wait()
        stage[...] = jnp.sum(first[...], 0)
        copies = [copy(stage, second.at[p], slot) for slot in range(strings - 1, len(peers))]
        for item in copies:
            item.start()
        second[p] = stage[...]
        for item in copies:
            item.wait()
        out_ref[...] = jnp.sum(second[...], 0)

    tile = local.shape
    return pl.pallas_call(
        kernel,
        out_shape=jax.ShapeDtypeStruct(tile, local.dtype),
        in_specs=[pl.BlockSpec(memory_space=pltpu.VMEM)],
        out_specs=pl.BlockSpec(memory_space=pltpu.VMEM),
        scratch_shapes=[
            pltpu.VMEM((strings,) + tile, local.dtype),
            pltpu.VMEM((planes,) + tile, local.dtype),
            pltpu.VMEM(tile, local.dtype),
            pltpu.SemaphoreType.DMA((strings + planes - 2,)),
            pltpu.SemaphoreType.DMA((strings + planes - 2,)),
        ],
        compiler_params=pltpu.CompilerParams(collective_id=ident, has_side_effects=True),
        name="sum_everywhere",
    )(local)


def halves(value):
    high = value.astype(jnp.bfloat16)
    return high, (value - high.astype(jnp.float32)).astype(jnp.bfloat16)


def left_factor(real, imag):
    real_high, real_low = halves(real)
    imag_high, imag_low = halves(imag)
    high = jnp.concatenate([real_high, imag_high], 1)
    return jnp.concatenate([high, high, real_low, imag_low], 1)


def right_factor(real, imag):
    real_high, real_low = halves(real)
    imag_high, imag_low = halves(imag)
    high = [
        jnp.concatenate([real_high, imag_high], 1),
        jnp.concatenate([-imag_high, real_high], 1),
    ]
    low = [
        jnp.concatenate([real_low, imag_low], 1),
        jnp.concatenate([-imag_low, real_low], 1),
    ]
    return jnp.concatenate(high + low + high, 0)


def newton_kernel(whole_ref, out_ref):
    real, imag = whole_ref[0].astype(jnp.float32), whole_ref[1].astype(jnp.float32)
    bands = real.shape[0]
    magnitude = jnp.sqrt(real * real + imag * imag)
    colmax = jnp.max(jnp.sum(magnitude, axis=0, keepdims=True), axis=1, keepdims=True)
    rowmax = jnp.max(jnp.sum(magnitude, axis=1, keepdims=True), axis=0, keepdims=True)
    factor = 1.0 / (colmax * rowmax + EPS_SCALE)
    x_re, x_im = real.T * factor, -imag.T * factor
    whole = left_factor(real, imag)
    for turn in range(NEWTON):
        p = jnp.dot(whole, right_factor(x_re, x_im), preferred_element_type=jnp.float32)
        q = jnp.dot(
            left_factor(x_re, x_im),
            right_factor(p[:, :bands], p[:, bands:]),
            preferred_element_type=jnp.float32,
        )
        x_re = 2.0 * x_re - q[:, :bands]
        x_im = 2.0 * x_im - q[:, bands:]
    out_ref[0] = x_re.astype(jnp.bfloat16)
    out_ref[1] = x_im.astype(jnp.bfloat16)


def newton_rounded(whole):
    return pl.pallas_call(
        newton_kernel,
        out_shape=jax.ShapeDtypeStruct(whole.shape, jnp.bfloat16),
        in_specs=[pl.BlockSpec(memory_space=pltpu.VMEM)],
        out_specs=pl.BlockSpec(memory_space=pltpu.VMEM),
        name="newton",
    )(whole)


def spread_body(strings, planes, states_re, states_im, gmap):
    _, bands, width = states_re.shape
    count = strings * planes
    piece = width // strings
    total_width = width * planes
    rows = 2 * bands // count
    half = count // 2
    share = bands // planes
    count_all = 2 * strings * bands * total_width
    bf16, f32 = jnp.bfloat16, jnp.float32

    def place():
        return lax.axis_index("kstr"), lax.axis_index("pw")

    def over_string(step):
        k, p = place()
        return (lax.rem(k + step, strings), p)

    def over_planes(step):
        k, p = place()
        return (k, lax.rem(p + step, planes))

    def over_all(step):
        k, p = place()
        peer = lax.rem(rank_of(k, p, planes) + step, count)
        return (peer // planes, lax.rem(peer, planes))

    def columns(index, size):
        return pl.ds(pl.multiple_of(index * size, size), size)

    def band_rows(rank):
        return pl.ds(pl.multiple_of(lax.rem(rank, half) * rows, rows), rows)

    def spread(refs, target):
        re, im, out = refs
        k, _ = place()
        cut = columns(target[0], piece)
        return [(re.at[:, cut], out.at[k, 0]), (im.at[:, cut], out.at[k, 1])]

    def collect(refs, target):
        new, re, im = refs
        k, _ = place()
        cut = columns(k, piece)
        return [(new.at[target[0], 0], re.at[:, cut]), (new.at[target[0], 1], im.at[:, cut])]

    def to_bands(refs, target):
        own, out = refs
        k, p = place()
        rank = rank_of(target[0], target[1], planes)
        which = (rank // half) * (strings - 1)
        return [(own.at[which, :, band_rows(rank), :], out.at[:, :, columns(p * strings + k, piece)])]

    def from_bands(refs, target):
        rolled, out = refs
        rank = rank_of(*place(), planes)
        block = target[1] * strings + target[0]
        return [(rolled.at[:, :, columns(block, piece)], out.at[rank // half, :, band_rows(rank), :])]

    def sum_string(refs, target):
        part, out = refs
        return [(part.at[target[0]], out.at[place()[0]])]

    def sum_planes(refs, target):
        part, out = refs
        return [(part.at[:, columns(target[1], share), :], out.at[place()[1]])]

    def gather_planes(refs, target):
        part, out = refs
        return [(part, out.at[:, columns(place()[1], share), :])]

    def gather_string(refs, target):
        part, out = refs
        return [(part, out.at[place()[0]])]

    here = place
    offset = jnp.mod(gmap[0] - lax.axis_index("pw") * width, total_width)
    back_offset = jnp.mod(total_width - offset, total_width)
    amount = jnp.where(rank_of(*place(), planes) < half, offset, back_offset)

    shape = jax.ShapeDtypeStruct
    states = exchange(
        "spread", 1, strings, here, over_string, spread,
        (states_re[0], states_im[0]), shape((strings, 2, bands, piece), bf16), 2,
    )
    for step in range(STEPS):
        banded = exchange(
            "to_bands", 2, count, here, over_all, to_bands,
            (states,), shape((2, rows, total_width), bf16),
        )
        rolled = lax.dynamic_slice_in_dim(
            jnp.concatenate([banded, banded], 2), amount, total_width, 2
        )
        turned = exchange(
            "from_bands", 3, count, here, over_all, from_bands,
            (rolled,), shape((2, 2, bands, piece), bf16),
        )
        following = jnp.concatenate([states[1:], turned[:1]], 0)
        before = jnp.concatenate([turned[1:], states[:-1]], 0)
        s_re = bf_product("kmg,kng->kmn", states[:, 0], following[:, 0]) + bf_product(
            "kmg,kng->kmn", states[:, 1], following[:, 1]
        )
        s_im = bf_product("kmg,kng->kmn", states[:, 0], following[:, 1]) - bf_product(
            "kmg,kng->kmn", states[:, 1], following[:, 0]
        )
        partial_value = (jnp.stack([s_re, s_im], 1) / total_width).astype(bf16)
        pieces = exchange(
            "sum_string", 4, strings, here, over_string, sum_string,
            (partial_value,), shape((strings, 2, bands, bands), bf16),
        )
        part = jnp.sum(pieces.astype(f32), 0).astype(bf16)
        pieces = exchange(
            "sum_planes", 5, planes, here, over_planes, sum_planes,
            (part,), shape((planes, 2, share, bands), bf16),
        )
        part = jnp.sum(pieces.astype(f32), 0).astype(bf16)
        whole = exchange(
            "gather_planes", 6, planes, here, over_planes, gather_planes,
            (part,), shape((2, bands, bands), bf16),
        )
        rounded = newton_rounded(whole)
        inverse = exchange(
            "gather_string", 7, strings, here, over_string, gather_string,
            (rounded,), shape((strings, 2, bands, bands), bf16),
        )
        earlier = jnp.concatenate([inverse[-1:], inverse[:-1]], 0)
        a_re = bf_product("kmn,kmg->kng", inverse[:, 0], following[:, 0]) - bf_product(
            "kmn,kmg->kng", inverse[:, 1], following[:, 1]
        )
        a_im = bf_product("kmn,kmg->kng", inverse[:, 0], following[:, 1]) + bf_product(
            "kmn,kmg->kng", inverse[:, 1], following[:, 0]
        )
        incoming = dual_terms(earlier, before).astype(f32)
        g_re = a_im - incoming[:, 1]
        g_im = incoming[:, 0] - a_re
        local = jnp.sum((g_re * g_re + g_im * g_im).reshape(-1, 8, piece // 128, 128), (0, 2))
        total = jnp.sum(sum_everywhere(8, strings, planes, local))
        rms = jnp.sqrt(total / count_all + EPS_NORM)
        new_re = (states[:, 0].astype(f32) + TAU_STEP * g_re / rms).astype(bf16)
        new_im = (states[:, 1].astype(f32) + TAU_STEP * g_im / rms).astype(bf16)
        states = jnp.stack([new_re, new_im], 1)
    new_re, new_im = exchange(
        "collect", 9, strings, here, over_string, collect,
        (states,), (shape((bands, width), bf16), shape((bands, width), bf16)), 2,
    )
    return (new_re[None], new_im[None])


def solution(mesh):
    placed = (P("kstr", None, "pw"), P("kstr", None, "pw"), P("pw"))
    strings, planes = mesh.shape["kstr"], mesh.shape["pw"]

    def body(states_re, states_im, gmap):
        kpoints, bands, width = states_re.shape
        count = strings * planes
        fits = (
            kpoints == 1
            and strings > 1
            and planes > 1
            and width % (strings * 128) == 0
            and bands % (planes * 16) == 0
            and (2 * bands) % (count * 16) == 0
        )
        if not fits:
            return general_body(states_re, states_im, gmap)
        return spread_body(strings, planes, states_re, states_im, gmap)

    return jax.shard_map(
        body,
        mesh=mesh,
        in_specs=placed,
        out_specs=(P("kstr", None, "pw"), P("kstr", None, "pw")),
        check_vma=False,
    )
```

```python
import functools

import jax
import jax.numpy as jnp
from jax import lax
from jax.experimental import pallas as pl
from jax.experimental.pallas import tpu as pltpu
from jax.sharding import PartitionSpec as P

NEWTON = 4
STEPS = 2


HIGH = lax.Precision.HIGHEST
EPS_SCALE = 1e-06
EPS_NORM = 1e-06
TAU_STEP = 0.25


def shifted(value, axis, by):
    count = lax.axis_size(axis)
    return lax.ppermute(value, axis, [(i, (i + by) % count) for i in range(count)])


def padded_2(block, sides, width):
    for axis, dim in sides:
        count = lax.axis_size(axis)
        forward = [(i, i + 1) for i in range(count - 1)]
        forward.append((count - 1, 0))
        backward = [(target, source) for source, target in forward]
        low = lax.ppermute(
            lax.slice_in_dim(block, block.shape[dim] - width, None, axis=dim), axis, forward
        )
        high = lax.ppermute(lax.slice_in_dim(block, 0, width, axis=dim), axis, backward)
        block = jnp.concatenate([low, block, high], axis=dim)
    return block


def complex_mul(left, right):

    def matmul(first, second):
        return jnp.einsum("kij,kjl->kil", first, second, precision=HIGH)

    real = matmul(left[:, 0], right[:, 0]) - matmul(left[:, 1], right[:, 1])
    imag = matmul(left[:, 0], right[:, 1]) + matmul(left[:, 1], right[:, 0])
    return jnp.stack([real, imag], 1)


def start_inverse(whole):
    magnitude = jnp.sqrt(whole[:, 0] * whole[:, 0] + whole[:, 1] * whole[:, 1])
    colmax = jnp.max(jnp.sum(magnitude, axis=1), axis=1)
    rowmax = jnp.max(jnp.sum(magnitude, axis=2), axis=1)
    factor = (1.0 / (colmax * rowmax + EPS_SCALE))[:, None, None]
    return jnp.stack(
        [jnp.swapaxes(whole[:, 0], 1, 2) * factor, -jnp.swapaxes(whole[:, 1], 1, 2) * factor], 1
    )


def newton_full(whole):
    iterate = start_inverse(whole)
    for turn in range(NEWTON):
        iterate = 2.0 * iterate - complex_mul(iterate, complex_mul(whole, iterate))
    return iterate


def bf_product(form, left, right):
    return jnp.einsum(form, left, right, preferred_element_type=jnp.float32)


def dual_terms(rounded, states):
    real = bf_product("kmn,kmg->kng", rounded[:, 0], states[:, 0]) + bf_product(
        "kmn,kmg->kng", rounded[:, 1], states[:, 1]
    )
    imag = bf_product("kmn,kmg->kng", rounded[:, 0], states[:, 1]) - bf_product(
        "kmn,kmg->kng", rounded[:, 1], states[:, 0]
    )
    return jnp.stack([real, imag], 1).astype(jnp.bfloat16)


def rotate_columns(block, amount, width):
    blocks_off = amount // width
    rest = amount % width
    plane_size = lax.axis_size("pw")
    for bit in range((plane_size - 1).bit_length()):
        moved = shifted(block, "pw", -(1 << bit))
        block = jnp.where(jnp.bitwise_and(jnp.right_shift(blocks_off, bit), 1) == 1, moved, block)
    after = shifted(block, "pw", -1)
    joined = jnp.concatenate([block, after], block.ndim - 1)
    return lax.dynamic_slice_in_dim(joined, rest, width, block.ndim - 1)


def general_body(states_re, states_im, gmap):
    kpoints, bands, width = states_re.shape
    string_size = lax.axis_size("kstr")
    plane_size = lax.axis_size("pw")
    string_index = lax.axis_index("kstr")
    total_width = width * plane_size
    offset = jnp.mod(gmap[0] - lax.axis_index("pw") * width, total_width)
    back_offset = jnp.mod(total_width - offset, total_width)
    at_first = string_index == 0
    at_last = string_index == string_size - 1
    count_all = 2 * kpoints * string_size * bands * width * plane_size
    states = jnp.stack([states_re, states_im], 1)
    for step in range(STEPS):
        padded = padded_2(states, (("kstr", 0),), 1)
        ahead = padded[-1:]
        behind = padded[:1]
        turned = rotate_columns(ahead, offset, width)
        ahead = jnp.where(at_last, turned, ahead)
        following = jnp.concatenate([states[1:], ahead], 0)
        s_re = bf_product("kmg,kng->kmn", states[:, 0], following[:, 0]) + bf_product(
            "kmg,kng->kmn", states[:, 1], following[:, 1]
        )
        s_im = bf_product("kmg,kng->kmn", states[:, 0], following[:, 1]) - bf_product(
            "kmg,kng->kmn", states[:, 1], following[:, 0]
        )
        partial_value = jnp.stack([s_re, s_im], 1)
        whole = lax.psum(partial_value, "pw") / (width * plane_size)
        inverse = newton_full(whole)
        rounded = inverse.astype(jnp.bfloat16)
        a_re = bf_product("kmn,kmg->kng", rounded[:, 0], following[:, 0]) - bf_product(
            "kmn,kmg->kng", rounded[:, 1], following[:, 1]
        )
        a_im = bf_product("kmn,kmg->kng", rounded[:, 0], following[:, 1]) + bf_product(
            "kmn,kmg->kng", rounded[:, 1], following[:, 0]
        )
        earlier = dual_terms(rounded[:-1], states[:-1])
        previous_inverse = shifted(rounded, "kstr", 1)
        arrived = dual_terms(previous_inverse, behind)
        placed = rotate_columns(arrived, back_offset, width)
        arrived = jnp.where(at_first, placed, arrived)
        incoming = jnp.concatenate([arrived, earlier], 0).astype(jnp.float32)
        g_re = a_im - incoming[:, 1]
        g_im = incoming[:, 0] - a_re
        total = lax.psum(jnp.sum(g_re * g_re + g_im * g_im), ("kstr", "pw"))
        rms = jnp.sqrt(total / count_all + EPS_NORM)
        new_re = (states[:, 0].astype(jnp.float32) + TAU_STEP * g_re / rms).astype(jnp.bfloat16)
        new_im = (states[:, 1].astype(jnp.float32) + TAU_STEP * g_im / rms).astype(jnp.bfloat16)
        states = jnp.stack([new_re, new_im], 1)
    return (states[:, 0], states[:, 1])


def exchange(name, ident, peers, here, there, copies, args, outs, parts=1):
    n_in = len(args)

    def kernel(*refs):
        data, (send, recv, local) = refs[:-3], refs[-3:]
        barrier = pltpu.get_barrier_semaphore()

        def greet(step, carry):
            pl.semaphore_signal(
                barrier, inc=1, device_id=there(step), device_id_type=pl.DeviceIdType.MESH
            )
            return carry

        lax.fori_loop(1, peers, greet, 0)
        pl.semaphore_wait(barrier, peers - 1)

        def remote(step):
            target = there(step)
            return [
                pltpu.make_async_remote_copy(
                    src_ref=source,
                    dst_ref=place,
                    send_sem=send.at[step, index],
                    recv_sem=recv.at[step, index],
                    device_id=target,
                    device_id_type=pl.DeviceIdType.MESH,
                )
                for index, (source, place) in enumerate(copies(data, target))
            ]

        def begin(step, carry):
            for copy in remote(step):
                copy.start()
            return carry

        def finish(step, carry):
            for copy in remote(step):
                copy.wait()
            return carry

        lax.fori_loop(1, peers, begin, 0)
        own = [
            pltpu.make_async_copy(source, place, local.at[index])
            for index, (source, place) in enumerate(copies(data, here()))
        ]
        for copy in own:
            copy.start()
        for copy in own:
            copy.wait()
        lax.fori_loop(1, peers, finish, 0)

    return pl.pallas_call(
        kernel,
        out_shape=outs,
        in_specs=[pl.BlockSpec(memory_space=pltpu.VMEM)] * n_in,
        out_specs=jax.tree.map(lambda _: pl.BlockSpec(memory_space=pltpu.VMEM), outs),
        scratch_shapes=[
            pltpu.SemaphoreType.DMA((peers, parts)),
            pltpu.SemaphoreType.DMA((peers, parts)),
            pltpu.SemaphoreType.DMA((parts,)),
        ],
        compiler_params=pltpu.CompilerParams(collective_id=ident, has_side_effects=True),
        name=name,
    )(*args)


def sum_everywhere(ident, strings, planes, local):
    def kernel(local_ref, out_ref, first, second, stage, send, recv):
        k, p = lax.axis_index("kstr"), lax.axis_index("pw")

        def string_peer(step):
            return (lax.rem(k + step, strings), p)

        def plane_peer(step):
            return (k, lax.rem(p + step, planes))

        barrier = pltpu.get_barrier_semaphore()
        peers = [string_peer(step) for step in range(1, strings)]
        peers += [plane_peer(step) for step in range(1, planes)]
        for peer in peers:
            pl.semaphore_signal(
                barrier, inc=1, device_id=peer, device_id_type=pl.DeviceIdType.MESH
            )
        pl.semaphore_wait(barrier, len(peers))

        def copy(source, place, slot):
            return pltpu.make_async_remote_copy(
                src_ref=source,
                dst_ref=place,
                send_sem=send.at[slot],
                recv_sem=recv.at[slot],
                device_id=peers[slot],
                device_id_type=pl.DeviceIdType.MESH,
            )

        copies = [copy(local_ref, first.at[k], slot) for slot in range(strings - 1)]
        for item in copies:
            item.start()
        first[k] = local_ref[...]
        for item in copies:
            item.wait()
        stage[...] = jnp.sum(first[...], 0)
        copies = [copy(stage, second.at[p], slot) for slot in range(strings - 1, len(peers))]
        for item in copies:
            item.start()
        second[p] = stage[...]
        for item in copies:
            item.wait()
        out_ref[...] = jnp.sum(second[...], 0)

    tile = local.shape
    return pl.pallas_call(
        kernel,
        out_shape=jax.ShapeDtypeStruct(tile, local.dtype),
        in_specs=[pl.BlockSpec(memory_space=pltpu.VMEM)],
        out_specs=pl.BlockSpec(memory_space=pltpu.VMEM),
        scratch_shapes=[
            pltpu.VMEM((strings,) + tile, local.dtype),
            pltpu.VMEM((planes,) + tile, local.dtype),
            pltpu.VMEM(tile, local.dtype),
            pltpu.SemaphoreType.DMA((strings + planes - 2,)),
            pltpu.SemaphoreType.DMA((strings + planes - 2,)),
        ],
        compiler_params=pltpu.CompilerParams(collective_id=ident, has_side_effects=True),
        name="sum_everywhere",
    )(local)


def halves(value):
    high = value.astype(jnp.bfloat16)
    return high, (value - high.astype(jnp.float32)).astype(jnp.bfloat16)


def left_factor(real, imag):
    real_high, real_low = halves(real)
    imag_high, imag_low = halves(imag)
    high = jnp.concatenate([real_high, imag_high], 1)
    return jnp.concatenate([high, high, real_low, imag_low], 1)


def right_factor(real, imag):
    real_high, real_low = halves(real)
    imag_high, imag_low = halves(imag)
    high = [
        jnp.concatenate([real_high, imag_high], 1),
        jnp.concatenate([-imag_high, real_high], 1),
    ]
    low = [
        jnp.concatenate([real_low, imag_low], 1),
        jnp.concatenate([-imag_low, real_low], 1),
    ]
    return jnp.concatenate(high + low + high, 0)


def newton_kernel(whole_ref, out_ref):
    real, imag = whole_ref[0].astype(jnp.float32), whole_ref[1].astype(jnp.float32)
    bands = real.shape[0]
    magnitude = jnp.sqrt(real * real + imag * imag)
    colmax = jnp.max(jnp.sum(magnitude, axis=0, keepdims=True), axis=1, keepdims=True)
    rowmax = jnp.max(jnp.sum(magnitude, axis=1, keepdims=True), axis=0, keepdims=True)
    factor = 1.0 / (colmax * rowmax + EPS_SCALE)
    x_re, x_im = real.T * factor, -imag.T * factor
    whole = left_factor(real, imag)
    for turn in range(NEWTON):
        p = jnp.dot(whole, right_factor(x_re, x_im), preferred_element_type=jnp.float32)
        q = jnp.dot(
            left_factor(x_re, x_im),
            right_factor(p[:, :bands], p[:, bands:]),
            preferred_element_type=jnp.float32,
        )
        x_re = 2.0 * x_re - q[:, :bands]
        x_im = 2.0 * x_im - q[:, bands:]
    out_ref[0] = x_re.astype(jnp.bfloat16)
    out_ref[1] = x_im.astype(jnp.bfloat16)


def newton_rounded(whole):
    return pl.pallas_call(
        newton_kernel,
        out_shape=jax.ShapeDtypeStruct(whole.shape, jnp.bfloat16),
        in_specs=[pl.BlockSpec(memory_space=pltpu.VMEM)],
        out_specs=pl.BlockSpec(memory_space=pltpu.VMEM),
        name="newton",
    )(whole)


def remote_copy(source, place, send, recv, target):
    return pltpu.make_async_remote_copy(
        src_ref=source,
        dst_ref=place,
        send_sem=send,
        recv_sem=recv,
        device_id=target,
        device_id_type=pl.DeviceIdType.MESH,
    )


def greet_all(greeted, awaited):
    barrier = pltpu.get_barrier_semaphore()
    for peer in greeted:
        pl.semaphore_signal(barrier, inc=1, device_id=peer, device_id_type=pl.DeviceIdType.MESH)
    pl.semaphore_wait(barrier, awaited)


def spread(strings, planes, states_re, states_im):
    bands, width = states_re.shape
    piece = width // strings

    def kernel(re_ref, im_ref, out_ref, joined_ref, send, recv, local):
        k, p = lax.axis_index("kstr"), lax.axis_index("pw")
        forward = (k < STEPS).astype(jnp.int32)
        giver = (k, lax.rem(p + planes - 1 + 2 * forward, planes))
        taker = (k, lax.rem(p + planes + 1 - 2 * forward, planes))
        string_peers = [(lax.rem(k + step, strings), p) for step in range(1, strings)]
        greet_all(string_peers + [giver], strings)
        kept = pl.ds(pl.multiple_of((1 - forward) * width, width), width)
        other = pl.ds(pl.multiple_of(forward * width, width), width)
        mine = pl.ds(pl.multiple_of(k * piece, piece), piece)
        copies, inside = [], []
        for part, ref in enumerate((re_ref, im_ref)):
            for slot, peer in enumerate(string_peers):
                cut = pl.ds(pl.multiple_of(peer[0] * piece, piece), piece)
                copies.append(
                    remote_copy(
                        ref.at[:, cut], out_ref.at[k, part], send.at[slot, part], recv.at[slot, part], peer
                    )
                )
            slot = strings - 1
            copies.append(
                remote_copy(
                    ref, joined_ref.at[part, :, other], send.at[slot, part], recv.at[slot, part], taker
                )
            )
            inside.append(
                pltpu.make_async_copy(ref, joined_ref.at[part, :, kept], local.at[0, part])
            )
            inside.append(
                pltpu.make_async_copy(ref.at[:, mine], out_ref.at[k, part], local.at[1, part])
            )
        for copy in copies + inside:
            copy.start()
        for copy in inside + copies:
            copy.wait()

    vmem = pl.BlockSpec(memory_space=pltpu.VMEM)
    return pl.pallas_call(
        kernel,
        out_shape=(
            jax.ShapeDtypeStruct((strings, 2, bands, piece), states_re.dtype),
            jax.ShapeDtypeStruct((2, bands, 2 * width), states_re.dtype),
        ),
        in_specs=[vmem, vmem],
        out_specs=(vmem, vmem),
        scratch_shapes=[
            pltpu.SemaphoreType.DMA((strings, 2)),
            pltpu.SemaphoreType.DMA((strings, 2)),
            pltpu.SemaphoreType.DMA((2, 2)),
        ],
        compiler_params=pltpu.CompilerParams(collective_id=1, has_side_effects=True),
        name="spread",
    )(states_re, states_im)


def turn_blocks(strings, planes, shift, aligned):
    _, bands, width = aligned.shape
    piece = width // strings

    def kernel(block_ref, out_ref, send, recv, local):
        k, p = lax.axis_index("kstr"), lax.axis_index("pw")
        up, down = lax.rem(p + shift, planes), lax.rem(p + planes - shift, planes)
        steps = range(1 if shift == 0 else 0, strings)
        forward = (k < STEPS).astype(jnp.int32)
        target_plane = forward * down + (1 - forward) * up
        givers, takers = [], []
        for step in steps:
            other = lax.rem(k + strings - step, strings)
            ahead = (other < STEPS).astype(jnp.int32)
            givers.append((other, ahead * up + (1 - ahead) * down))
            takers.append((lax.rem(k + step, strings), target_plane))
        greet_all(givers, len(takers))
        copies = []
        for slot, taker in enumerate(takers):
            cut = pl.ds(pl.multiple_of(taker[0] * piece, piece), piece)
            copies.append(
                remote_copy(
                    block_ref.at[:, :, cut], out_ref.at[k], send.at[slot], recv.at[slot], taker
                )
            )
        for copy in copies:
            copy.start()
        if shift == 0:
            cut = pl.ds(pl.multiple_of(k * piece, piece), piece)
            inside = pltpu.make_async_copy(block_ref.at[:, :, cut], out_ref.at[k], local.at[0])
            inside.start()
            inside.wait()
        for copy in copies:
            copy.wait()

    vmem = pl.BlockSpec(memory_space=pltpu.VMEM)
    return pl.pallas_call(
        kernel,
        out_shape=jax.ShapeDtypeStruct((strings, 2, bands, piece), aligned.dtype),
        in_specs=[vmem],
        out_specs=vmem,
        scratch_shapes=[
            pltpu.SemaphoreType.DMA((strings,)),
            pltpu.SemaphoreType.DMA((strings,)),
            pltpu.SemaphoreType.DMA((1,)),
        ],
        compiler_params=pltpu.CompilerParams(collective_id=20 + shift, has_side_effects=True),
        name=f"turn_{shift}",
    )(aligned)


def spread_body(strings, planes, states_re, states_im, gmap):
    _, bands, width = states_re.shape
    piece = width // strings
    total_width = width * planes
    share = bands // planes
    count_all = 2 * strings * bands * total_width
    bf16, f32 = jnp.bfloat16, jnp.float32

    def place():
        return lax.axis_index("kstr"), lax.axis_index("pw")

    def over_string(step):
        k, p = place()
        return (lax.rem(k + step, strings), p)

    def over_planes(step):
        k, p = place()
        return (k, lax.rem(p + step, planes))

    def columns(index, size):
        return pl.ds(pl.multiple_of(index * size, size), size)

    def collect(refs, target):
        new, re, im = refs
        k, _ = place()
        cut = columns(k, piece)
        return [(new.at[target[0], 0], re.at[:, cut]), (new.at[target[0], 1], im.at[:, cut])]

    def sum_string(refs, target):
        part, out = refs
        return [(part.at[target[0]], out.at[place()[0]])]

    def sum_planes(refs, target):
        part, out = refs
        return [(part.at[:, columns(target[1], share), :], out.at[place()[1]])]

    def gather_planes(refs, target):
        part, out = refs
        return [(part, out.at[:, columns(place()[1], share), :])]

    def gather_string(refs, target):
        part, out = refs
        return [(part, out.at[place()[0]])]

    here = place
    offset = jnp.mod(gmap[0] - lax.axis_index("pw") * width, total_width)
    shape = jax.ShapeDtypeStruct
    states, joined = spread(strings, planes, states_re[0], states_im[0])
    blocks_off, rest = offset // width, jnp.mod(offset, width)
    start = jnp.where(lax.axis_index("kstr") < STEPS, rest, width - rest)
    aligned = lax.dynamic_slice_in_dim(joined, start, width, 2)
    halo = lax.switch(
        blocks_off,
        [functools.partial(turn_blocks, strings, planes, shift) for shift in range(planes)],
        aligned,
    )
    chain = jnp.concatenate([halo[strings - STEPS :], states, halo[:STEPS]], 0)
    for step in range(STEPS):
        wide = STEPS - 1 - step
        own = chain[wide + 1 : wide + 1 + strings]
        ahead = chain[wide + 2 : wide + 2 + strings]
        s_re = bf_product("kmg,kng->kmn", own[:, 0], ahead[:, 0]) + bf_product(
            "kmg,kng->kmn", own[:, 1], ahead[:, 1]
        )
        s_im = bf_product("kmg,kng->kmn", own[:, 0], ahead[:, 1]) - bf_product(
            "kmg,kng->kmn", own[:, 1], ahead[:, 0]
        )
        partial_value = (jnp.stack([s_re, s_im], 1) / total_width).astype(bf16)
        pieces = exchange(
            "sum_string", 4, strings, here, over_string, sum_string,
            (partial_value,), shape((strings, 2, bands, bands), bf16),
        )
        part = jnp.sum(pieces.astype(f32), 0).astype(bf16)
        pieces = exchange(
            "sum_planes", 5, planes, here, over_planes, sum_planes,
            (part,), shape((planes, 2, share, bands), bf16),
        )
        part = jnp.sum(pieces.astype(f32), 0).astype(bf16)
        whole = exchange(
            "gather_planes", 6, planes, here, over_planes, gather_planes,
            (part,), shape((2, bands, bands), bf16),
        )
        rounded = newton_rounded(whole)
        inverse = exchange(
            "gather_string", 7, strings, here, over_string, gather_string,
            (rounded,), shape((strings, 2, bands, bands), bf16),
        )
        links = jnp.stack(
            [inverse[(link - wide - 1) % strings] for link in range(strings + 2 * wide + 1)], 0
        )
        inverse, earlier = links[1:], links[:-1]
        states, following, before = chain[1:-1], chain[2:], chain[:-2]
        a_re = bf_product("kmn,kmg->kng", inverse[:, 0], following[:, 0]) - bf_product(
            "kmn,kmg->kng", inverse[:, 1], following[:, 1]
        )
        a_im = bf_product("kmn,kmg->kng", inverse[:, 0], following[:, 1]) + bf_product(
            "kmn,kmg->kng", inverse[:, 1], following[:, 0]
        )
        incoming = dual_terms(earlier, before).astype(f32)
        g_re = a_im - incoming[:, 1]
        g_im = incoming[:, 0] - a_re
        kept_re, kept_im = g_re[wide : wide + strings], g_im[wide : wide + strings]
        local = jnp.sum((kept_re * kept_re + kept_im * kept_im).reshape(-1, 8, piece // 128, 128), (0, 2))
        total = jnp.sum(sum_everywhere(8, strings, planes, local))
        rms = jnp.sqrt(total / count_all + EPS_NORM)
        new_re = (states[:, 0].astype(f32) + TAU_STEP * g_re / rms).astype(bf16)
        new_im = (states[:, 1].astype(f32) + TAU_STEP * g_im / rms).astype(bf16)
        chain = jnp.stack([new_re, new_im], 1)
    new_re, new_im = exchange(
        "collect", 9, strings, here, over_string, collect,
        (chain,), (shape((bands, width), bf16), shape((bands, width), bf16)), 2,
    )
    return (new_re[None], new_im[None])


def solution(mesh):
    placed = (P("kstr", None, "pw"), P("kstr", None, "pw"), P("pw"))
    strings, planes = mesh.shape["kstr"], mesh.shape["pw"]

    def body(states_re, states_im, gmap):
        kpoints, bands, width = states_re.shape
        fits = (
            kpoints == 1
            and strings > 1
            and planes > 1
            and width % (strings * 128) == 0
            and bands % (planes * 16) == 0
            and strings == 2 * STEPS
        )
        if not fits:
            return general_body(states_re, states_im, gmap)
        return spread_body(strings, planes, states_re, states_im, gmap)

    return jax.shard_map(
        body,
        mesh=mesh,
        in_specs=placed,
        out_specs=(P("kstr", None, "pw"), P("kstr", None, "pw")),
        check_vma=False,
    )
```

```python
import functools

import jax
import jax.numpy as jnp
from jax import lax
from jax.experimental import pallas as pl
from jax.experimental.pallas import tpu as pltpu
from jax.sharding import PartitionSpec as P

NEWTON = 4
STEPS = 2


HIGH = lax.Precision.HIGHEST
EPS_SCALE = 1e-06
EPS_NORM = 1e-06
TAU_STEP = 0.25


def shifted(value, axis, by):
    count = lax.axis_size(axis)
    return lax.ppermute(value, axis, [(i, (i + by) % count) for i in range(count)])


def padded_2(block, sides, width):
    for axis, dim in sides:
        count = lax.axis_size(axis)
        forward = [(i, i + 1) for i in range(count - 1)]
        forward.append((count - 1, 0))
        backward = [(target, source) for source, target in forward]
        low = lax.ppermute(
            lax.slice_in_dim(block, block.shape[dim] - width, None, axis=dim), axis, forward
        )
        high = lax.ppermute(lax.slice_in_dim(block, 0, width, axis=dim), axis, backward)
        block = jnp.concatenate([low, block, high], axis=dim)
    return block


def complex_mul(left, right):

    def matmul(first, second):
        return jnp.einsum("kij,kjl->kil", first, second, precision=HIGH)

    real = matmul(left[:, 0], right[:, 0]) - matmul(left[:, 1], right[:, 1])
    imag = matmul(left[:, 0], right[:, 1]) + matmul(left[:, 1], right[:, 0])
    return jnp.stack([real, imag], 1)


def start_inverse(whole):
    magnitude = jnp.sqrt(whole[:, 0] * whole[:, 0] + whole[:, 1] * whole[:, 1])
    colmax = jnp.max(jnp.sum(magnitude, axis=1), axis=1)
    rowmax = jnp.max(jnp.sum(magnitude, axis=2), axis=1)
    factor = (1.0 / (colmax * rowmax + EPS_SCALE))[:, None, None]
    return jnp.stack(
        [jnp.swapaxes(whole[:, 0], 1, 2) * factor, -jnp.swapaxes(whole[:, 1], 1, 2) * factor], 1
    )


def newton_full(whole):
    iterate = start_inverse(whole)
    for turn in range(NEWTON):
        iterate = 2.0 * iterate - complex_mul(iterate, complex_mul(whole, iterate))
    return iterate


def bf_product(form, left, right):
    return jnp.einsum(form, left, right, preferred_element_type=jnp.float32)


def dual_terms(rounded, states):
    real = bf_product("kmn,kmg->kng", rounded[:, 0], states[:, 0]) + bf_product(
        "kmn,kmg->kng", rounded[:, 1], states[:, 1]
    )
    imag = bf_product("kmn,kmg->kng", rounded[:, 0], states[:, 1]) - bf_product(
        "kmn,kmg->kng", rounded[:, 1], states[:, 0]
    )
    return jnp.stack([real, imag], 1).astype(jnp.bfloat16)


def rotate_columns(block, amount, width):
    blocks_off = amount // width
    rest = amount % width
    plane_size = lax.axis_size("pw")
    for bit in range((plane_size - 1).bit_length()):
        moved = shifted(block, "pw", -(1 << bit))
        block = jnp.where(jnp.bitwise_and(jnp.right_shift(blocks_off, bit), 1) == 1, moved, block)
    after = shifted(block, "pw", -1)
    joined = jnp.concatenate([block, after], block.ndim - 1)
    return lax.dynamic_slice_in_dim(joined, rest, width, block.ndim - 1)


def general_body(states_re, states_im, gmap):
    kpoints, bands, width = states_re.shape
    string_size = lax.axis_size("kstr")
    plane_size = lax.axis_size("pw")
    string_index = lax.axis_index("kstr")
    total_width = width * plane_size
    offset = jnp.mod(gmap[0] - lax.axis_index("pw") * width, total_width)
    back_offset = jnp.mod(total_width - offset, total_width)
    at_first = string_index == 0
    at_last = string_index == string_size - 1
    count_all = 2 * kpoints * string_size * bands * width * plane_size
    states = jnp.stack([states_re, states_im], 1)
    for step in range(STEPS):
        padded = padded_2(states, (("kstr", 0),), 1)
        ahead = padded[-1:]
        behind = padded[:1]
        turned = rotate_columns(ahead, offset, width)
        ahead = jnp.where(at_last, turned, ahead)
        following = jnp.concatenate([states[1:], ahead], 0)
        s_re = bf_product("kmg,kng->kmn", states[:, 0], following[:, 0]) + bf_product(
            "kmg,kng->kmn", states[:, 1], following[:, 1]
        )
        s_im = bf_product("kmg,kng->kmn", states[:, 0], following[:, 1]) - bf_product(
            "kmg,kng->kmn", states[:, 1], following[:, 0]
        )
        partial_value = jnp.stack([s_re, s_im], 1)
        whole = lax.psum(partial_value, "pw") / (width * plane_size)
        inverse = newton_full(whole)
        rounded = inverse.astype(jnp.bfloat16)
        a_re = bf_product("kmn,kmg->kng", rounded[:, 0], following[:, 0]) - bf_product(
            "kmn,kmg->kng", rounded[:, 1], following[:, 1]
        )
        a_im = bf_product("kmn,kmg->kng", rounded[:, 0], following[:, 1]) + bf_product(
            "kmn,kmg->kng", rounded[:, 1], following[:, 0]
        )
        earlier = dual_terms(rounded[:-1], states[:-1])
        previous_inverse = shifted(rounded, "kstr", 1)
        arrived = dual_terms(previous_inverse, behind)
        placed = rotate_columns(arrived, back_offset, width)
        arrived = jnp.where(at_first, placed, arrived)
        incoming = jnp.concatenate([arrived, earlier], 0).astype(jnp.float32)
        g_re = a_im - incoming[:, 1]
        g_im = incoming[:, 0] - a_re
        total = lax.psum(jnp.sum(g_re * g_re + g_im * g_im), ("kstr", "pw"))
        rms = jnp.sqrt(total / count_all + EPS_NORM)
        new_re = (states[:, 0].astype(jnp.float32) + TAU_STEP * g_re / rms).astype(jnp.bfloat16)
        new_im = (states[:, 1].astype(jnp.float32) + TAU_STEP * g_im / rms).astype(jnp.bfloat16)
        states = jnp.stack([new_re, new_im], 1)
    return (states[:, 0], states[:, 1])


def exchange(name, ident, peers, here, there, copies, args, outs, parts=1):
    n_in = len(args)

    def kernel(*refs):
        data, (send, recv, local) = refs[:-3], refs[-3:]
        barrier = pltpu.get_barrier_semaphore()

        def greet(step, carry):
            pl.semaphore_signal(
                barrier, inc=1, device_id=there(step), device_id_type=pl.DeviceIdType.MESH
            )
            return carry

        lax.fori_loop(1, peers, greet, 0)
        pl.semaphore_wait(barrier, peers - 1)

        def remote(step):
            target = there(step)
            return [
                pltpu.make_async_remote_copy(
                    src_ref=source,
                    dst_ref=place,
                    send_sem=send.at[step, index],
                    recv_sem=recv.at[step, index],
                    device_id=target,
                    device_id_type=pl.DeviceIdType.MESH,
                )
                for index, (source, place) in enumerate(copies(data, target))
            ]

        def begin(step, carry):
            for copy in remote(step):
                copy.start()
            return carry

        def finish(step, carry):
            for copy in remote(step):
                copy.wait()
            return carry

        lax.fori_loop(1, peers, begin, 0)
        own = [
            pltpu.make_async_copy(source, place, local.at[index])
            for index, (source, place) in enumerate(copies(data, here()))
        ]
        for copy in own:
            copy.start()
        for copy in own:
            copy.wait()
        lax.fori_loop(1, peers, finish, 0)

    return pl.pallas_call(
        kernel,
        out_shape=outs,
        in_specs=[pl.BlockSpec(memory_space=pltpu.VMEM)] * n_in,
        out_specs=jax.tree.map(lambda _: pl.BlockSpec(memory_space=pltpu.VMEM), outs),
        scratch_shapes=[
            pltpu.SemaphoreType.DMA((peers, parts)),
            pltpu.SemaphoreType.DMA((peers, parts)),
            pltpu.SemaphoreType.DMA((parts,)),
        ],
        compiler_params=pltpu.CompilerParams(collective_id=ident, has_side_effects=True),
        name=name,
    )(*args)


def sum_everywhere(ident, strings, planes, local):
    def kernel(local_ref, out_ref, first, second, stage, send, recv):
        k, p = lax.axis_index("kstr"), lax.axis_index("pw")

        def string_peer(step):
            return (lax.rem(k + step, strings), p)

        def plane_peer(step):
            return (k, lax.rem(p + step, planes))

        barrier = pltpu.get_barrier_semaphore()
        peers = [string_peer(step) for step in range(1, strings)]
        peers += [plane_peer(step) for step in range(1, planes)]
        for peer in peers:
            pl.semaphore_signal(
                barrier, inc=1, device_id=peer, device_id_type=pl.DeviceIdType.MESH
            )
        pl.semaphore_wait(barrier, len(peers))

        def copy(source, place, slot):
            return pltpu.make_async_remote_copy(
                src_ref=source,
                dst_ref=place,
                send_sem=send.at[slot],
                recv_sem=recv.at[slot],
                device_id=peers[slot],
                device_id_type=pl.DeviceIdType.MESH,
            )

        copies = [copy(local_ref, first.at[k], slot) for slot in range(strings - 1)]
        for item in copies:
            item.start()
        first[k] = local_ref[...]
        for item in copies:
            item.wait()
        stage[...] = jnp.sum(first[...], 0)
        copies = [copy(stage, second.at[p], slot) for slot in range(strings - 1, len(peers))]
        for item in copies:
            item.start()
        second[p] = stage[...]
        for item in copies:
            item.wait()
        out_ref[...] = jnp.sum(second[...], 0)

    tile = local.shape
    return pl.pallas_call(
        kernel,
        out_shape=jax.ShapeDtypeStruct(tile, local.dtype),
        in_specs=[pl.BlockSpec(memory_space=pltpu.VMEM)],
        out_specs=pl.BlockSpec(memory_space=pltpu.VMEM),
        scratch_shapes=[
            pltpu.VMEM((strings,) + tile, local.dtype),
            pltpu.VMEM((planes,) + tile, local.dtype),
            pltpu.VMEM(tile, local.dtype),
            pltpu.SemaphoreType.DMA((strings + planes - 2,)),
            pltpu.SemaphoreType.DMA((strings + planes - 2,)),
        ],
        compiler_params=pltpu.CompilerParams(collective_id=ident, has_side_effects=True),
        name="sum_everywhere",
    )(local)


def halves(value):
    high = value.astype(jnp.bfloat16)
    return high, (value - high.astype(jnp.float32)).astype(jnp.bfloat16)


def left_factor(real, imag):
    real_high, real_low = halves(real)
    imag_high, imag_low = halves(imag)
    high = jnp.concatenate([real_high, imag_high], 1)
    return jnp.concatenate([high, high, real_low, imag_low], 1)


def right_factor(real, imag):
    real_high, real_low = halves(real)
    imag_high, imag_low = halves(imag)
    high = [
        jnp.concatenate([real_high, imag_high], 1),
        jnp.concatenate([-imag_high, real_high], 1),
    ]
    low = [
        jnp.concatenate([real_low, imag_low], 1),
        jnp.concatenate([-imag_low, real_low], 1),
    ]
    return jnp.concatenate(high + low + high, 0)


def newton_rounded(real, imag):
    bands = real.shape[0]
    magnitude = jnp.sqrt(real * real + imag * imag)
    colmax = jnp.max(jnp.sum(magnitude, axis=0, keepdims=True), axis=1, keepdims=True)
    rowmax = jnp.max(jnp.sum(magnitude, axis=1, keepdims=True), axis=0, keepdims=True)
    factor = 1.0 / (colmax * rowmax + EPS_SCALE)
    x_re, x_im = real.T * factor, -imag.T * factor
    whole = left_factor(real, imag)
    for turn in range(NEWTON):
        p = jnp.dot(whole, right_factor(x_re, x_im), preferred_element_type=jnp.float32)
        q = jnp.dot(
            left_factor(x_re, x_im),
            right_factor(p[:, :bands], p[:, bands:]),
            preferred_element_type=jnp.float32,
        )
        x_re = 2.0 * x_re - q[:, :bands]
        x_im = 2.0 * x_im - q[:, bands:]
    return x_re.astype(jnp.bfloat16), x_im.astype(jnp.bfloat16)


def remote_copy(source, place, send, recv, target):
    return pltpu.make_async_remote_copy(
        src_ref=source,
        dst_ref=place,
        send_sem=send,
        recv_sem=recv,
        device_id=target,
        device_id_type=pl.DeviceIdType.MESH,
    )


def greet_all(greeted, awaited):
    barrier = pltpu.get_barrier_semaphore()
    for peer in greeted:
        pl.semaphore_signal(barrier, inc=1, device_id=peer, device_id_type=pl.DeviceIdType.MESH)
    pl.semaphore_wait(barrier, awaited)


def spread(strings, planes, states_re, states_im):
    bands, width = states_re.shape
    piece = width // strings

    def kernel(re_ref, im_ref, out_ref, joined_ref, send, recv, local):
        k, p = lax.axis_index("kstr"), lax.axis_index("pw")
        forward = (k < STEPS).astype(jnp.int32)
        giver = (k, lax.rem(p + planes - 1 + 2 * forward, planes))
        taker = (k, lax.rem(p + planes + 1 - 2 * forward, planes))
        string_peers = [(lax.rem(k + step, strings), p) for step in range(1, strings)]
        greet_all(string_peers + [giver], strings)
        kept = pl.ds(pl.multiple_of((1 - forward) * width, width), width)
        other = pl.ds(pl.multiple_of(forward * width, width), width)
        mine = pl.ds(pl.multiple_of(k * piece, piece), piece)
        copies, inside = [], []
        for part, ref in enumerate((re_ref, im_ref)):
            for slot, peer in enumerate(string_peers):
                cut = pl.ds(pl.multiple_of(peer[0] * piece, piece), piece)
                copies.append(
                    remote_copy(
                        ref.at[:, cut], out_ref.at[k, part], send.at[slot, part], recv.at[slot, part], peer
                    )
                )
            slot = strings - 1
            copies.append(
                remote_copy(
                    ref, joined_ref.at[part, :, other], send.at[slot, part], recv.at[slot, part], taker
                )
            )
            inside.append(
                pltpu.make_async_copy(ref, joined_ref.at[part, :, kept], local.at[0, part])
            )
            inside.append(
                pltpu.make_async_copy(ref.at[:, mine], out_ref.at[k, part], local.at[1, part])
            )
        for copy in copies + inside:
            copy.start()
        for copy in inside + copies:
            copy.wait()

    vmem = pl.BlockSpec(memory_space=pltpu.VMEM)
    return pl.pallas_call(
        kernel,
        out_shape=(
            jax.ShapeDtypeStruct((strings, 2, bands, piece), states_re.dtype),
            jax.ShapeDtypeStruct((2, bands, 2 * width), states_re.dtype),
        ),
        in_specs=[vmem, vmem],
        out_specs=(vmem, vmem),
        scratch_shapes=[
            pltpu.SemaphoreType.DMA((strings, 2)),
            pltpu.SemaphoreType.DMA((strings, 2)),
            pltpu.SemaphoreType.DMA((2, 2)),
        ],
        compiler_params=pltpu.CompilerParams(collective_id=1, has_side_effects=True),
        name="spread",
    )(states_re, states_im)


def turn_blocks(strings, planes, shift, aligned):
    _, bands, width = aligned.shape
    piece = width // strings

    def kernel(block_ref, out_ref, send, recv, local):
        k, p = lax.axis_index("kstr"), lax.axis_index("pw")
        up, down = lax.rem(p + shift, planes), lax.rem(p + planes - shift, planes)
        steps = range(1 if shift == 0 else 0, strings)
        forward = (k < STEPS).astype(jnp.int32)
        target_plane = forward * down + (1 - forward) * up
        givers, takers = [], []
        for step in steps:
            other = lax.rem(k + strings - step, strings)
            ahead = (other < STEPS).astype(jnp.int32)
            givers.append((other, ahead * up + (1 - ahead) * down))
            takers.append((lax.rem(k + step, strings), target_plane))
        greet_all(givers, len(takers))
        copies = []
        for slot, taker in enumerate(takers):
            cut = pl.ds(pl.multiple_of(taker[0] * piece, piece), piece)
            copies.append(
                remote_copy(
                    block_ref.at[:, :, cut], out_ref.at[k], send.at[slot], recv.at[slot], taker
                )
            )
        for copy in copies:
            copy.start()
        if shift == 0:
            cut = pl.ds(pl.multiple_of(k * piece, piece), piece)
            inside = pltpu.make_async_copy(block_ref.at[:, :, cut], out_ref.at[k], local.at[0])
            inside.start()
            inside.wait()
        for copy in copies:
            copy.wait()

    vmem = pl.BlockSpec(memory_space=pltpu.VMEM)
    return pl.pallas_call(
        kernel,
        out_shape=jax.ShapeDtypeStruct((strings, 2, bands, piece), aligned.dtype),
        in_specs=[vmem],
        out_specs=vmem,
        scratch_shapes=[
            pltpu.SemaphoreType.DMA((strings,)),
            pltpu.SemaphoreType.DMA((strings,)),
            pltpu.SemaphoreType.DMA((1,)),
        ],
        compiler_params=pltpu.CompilerParams(collective_id=20 + shift, has_side_effects=True),
        name=f"turn_{shift}",
    )(aligned)


def margin_of(own, ahead):
    left = jnp.concatenate([own[0], own[1]], 1)
    form = (((1,), (1,)), ((), ()))
    real = lax.dot_general(
        left, jnp.concatenate([ahead[0], ahead[1]], 1), form, preferred_element_type=jnp.float32
    )
    imag = lax.dot_general(
        left, jnp.concatenate([ahead[1], -ahead[0]], 1), form, preferred_element_type=jnp.float32
    )
    return real, imag


def inverses(ident, strings, planes, wide, total_width, chain):
    bands = chain.shape[2]
    share, middle = bands // planes, bands // 2
    chunks = bands // 128
    bf16, f32 = jnp.bfloat16, jnp.float32

    def kernel(chain_ref, out_ref, part, got_string, summed, got_planes, block, whole, rounded, *sems):
        send1, recv1, send2, recv2, send3, recv3, send4, recv4, send5, recv5 = sems
        k, p = lax.axis_index("kstr"), lax.axis_index("pw")
        string_peers = [(lax.rem(k + step, strings), p) for step in range(1, strings)]
        plane_peers = [(k, lax.rem(p + step, planes)) for step in range(1, planes)]
        side = lax.rem(p, 2)
        sibling = (k, p + 1 - 2 * side)

        def rows(index, size):
            return pl.ds(pl.multiple_of(index * size, size), size)

        barrier = pltpu.get_barrier_semaphore()
        for peer in string_peers + plane_peers:
            pl.semaphore_signal(
                barrier, inc=1, device_id=peer, device_id_type=pl.DeviceIdType.MESH
            )

        def put_margin(slot, which):
            real, imag = margin_of(chain_ref[wide + 1 + which], chain_ref[wide + 2 + which])
            part[slot, 0] = (real * (1.0 / total_width)).astype(bf16)
            part[slot, 1] = (imag * (1.0 / total_width)).astype(bf16)

        cuts = [pl.ds(chunk * 128, 128) for chunk in range(chunks)]
        over_string = []
        for slot, peer in enumerate(string_peers):
            put_margin(slot, peer[0])
            if slot == 0:
                pl.semaphore_wait(barrier, len(string_peers) + len(plane_peers))
            for chunk, cut in enumerate(cuts):
                copy = remote_copy(
                    part.at[slot, :, :, cut], got_string.at[slot, :, :, cut],
                    send1.at[slot, chunk], recv1.at[slot, chunk], peer,
                )
                copy.start()
                over_string.append((chunk, copy))
        put_margin(strings - 1, k)

        over_planes = []
        for chunk, cut in enumerate(cuts):
            for number, copy in over_string:
                if number == chunk:
                    copy.wait()
            total = part[strings - 1, :, :, cut].astype(f32)
            for slot in range(strings - 1):
                total = total + got_string[slot, :, :, cut].astype(f32)
            summed[:, :, cut] = total.astype(bf16)
            for slot, peer in enumerate(plane_peers):
                copy = remote_copy(
                    summed.at[:, rows(peer[1], share), cut], got_planes.at[slot, :, :, cut],
                    send2.at[slot, chunk], recv2.at[slot, chunk], peer,
                )
                copy.start()
                over_planes.append((chunk, copy))
        back = []
        for chunk, cut in enumerate(cuts):
            for number, copy in over_planes:
                if number == chunk:
                    copy.wait()
            total = summed[:, rows(p, share), cut].astype(f32)
            for slot in range(planes - 1):
                total = total + got_planes[slot, :, :, cut].astype(f32)
            block[:, :, cut] = total.astype(bf16)
            for slot, peer in enumerate(plane_peers):
                copy = remote_copy(
                    block.at[:, :, cut], whole.at[:, rows(p, share), cut],
                    send3.at[slot, chunk], recv3.at[slot, chunk], peer,
                )
                copy.start()
                back.append(copy)
            whole[:, rows(p, share), cut] = block[:, :, cut]
        for copy in back:
            copy.wait()

        real, imag = newton_rounded(whole[0].astype(f32), whole[1].astype(f32))
        rounded[0] = real
        rounded[1] = imag
        mine = rows(side, middle)
        first = []
        for slot, peer in enumerate(string_peers):
            copy = remote_copy(
                rounded.at[:, mine, :], out_ref.at[k, :, mine, :],
                send4.at[slot], recv4.at[slot], peer,
            )
            copy.start()
            first.append(copy)
        out_ref[k, 0] = real
        out_ref[k, 1] = imag
        second = []
        for slot, copy in enumerate(first):
            copy.wait()
            source = lax.rem(k + strings - slot - 1, strings)
            relay = remote_copy(
                out_ref.at[source, :, mine, :], out_ref.at[source, :, mine, :],
                send5.at[slot], recv5.at[slot], sibling,
            )
            relay.start()
            second.append(relay)
        for relay in second:
            relay.wait()

    vmem = pl.BlockSpec(memory_space=pltpu.VMEM)
    square = (2, bands, bands)
    dma = pltpu.SemaphoreType.DMA
    return pl.pallas_call(
        kernel,
        out_shape=jax.ShapeDtypeStruct((strings,) + square, bf16),
        in_specs=[vmem],
        out_specs=vmem,
        scratch_shapes=[
            pltpu.VMEM((strings,) + square, bf16),
            pltpu.VMEM((strings - 1,) + square, bf16),
            pltpu.VMEM(square, bf16),
            pltpu.VMEM((planes - 1, 2, share, bands), bf16),
            pltpu.VMEM((2, share, bands), bf16),
            pltpu.VMEM(square, bf16),
            pltpu.VMEM(square, bf16),
        ]
        + [dma((strings - 1, chunks))] * 2
        + [dma((planes - 1, chunks))] * 4
        + [dma((strings - 1,))] * 4,
        compiler_params=pltpu.CompilerParams(collective_id=ident, has_side_effects=True),
        name=f"inverses_{wide}",
    )(chain)


def spread_body(strings, planes, states_re, states_im, gmap):
    _, bands, width = states_re.shape
    piece = width // strings
    total_width = width * planes
    count_all = 2 * strings * bands * total_width
    bf16, f32 = jnp.bfloat16, jnp.float32

    def place():
        return lax.axis_index("kstr"), lax.axis_index("pw")

    def over_string(step):
        k, p = place()
        return (lax.rem(k + step, strings), p)

    def columns(index, size):
        return pl.ds(pl.multiple_of(index * size, size), size)

    def collect(refs, target):
        new, re, im = refs
        k, _ = place()
        cut = columns(k, piece)
        return [(new.at[target[0], 0], re.at[:, cut]), (new.at[target[0], 1], im.at[:, cut])]

    here = place
    offset = jnp.mod(gmap[0] - lax.axis_index("pw") * width, total_width)
    shape = jax.ShapeDtypeStruct
    states, joined = spread(strings, planes, states_re[0], states_im[0])
    blocks_off, rest = offset // width, jnp.mod(offset, width)
    start = jnp.where(lax.axis_index("kstr") < STEPS, rest, width - rest)
    aligned = lax.dynamic_slice_in_dim(joined, start, width, 2)
    halo = lax.switch(
        blocks_off,
        [functools.partial(turn_blocks, strings, planes, shift) for shift in range(planes)],
        aligned,
    )
    chain = jnp.concatenate([halo[strings - STEPS :], states, halo[:STEPS]], 0)
    for step in range(STEPS):
        wide = STEPS - 1 - step
        inverse = inverses(4 + step, strings, planes, wide, total_width, chain)
        links = jnp.stack(
            [inverse[(link - wide - 1) % strings] for link in range(strings + 2 * wide + 1)], 0
        )
        inverse, earlier = links[1:], links[:-1]
        states, following, before = chain[1:-1], chain[2:], chain[:-2]
        a_re = bf_product("kmn,kmg->kng", inverse[:, 0], following[:, 0]) - bf_product(
            "kmn,kmg->kng", inverse[:, 1], following[:, 1]
        )
        a_im = bf_product("kmn,kmg->kng", inverse[:, 0], following[:, 1]) + bf_product(
            "kmn,kmg->kng", inverse[:, 1], following[:, 0]
        )
        incoming = dual_terms(earlier, before).astype(f32)
        g_re = a_im - incoming[:, 1]
        g_im = incoming[:, 0] - a_re
        kept_re, kept_im = g_re[wide : wide + strings], g_im[wide : wide + strings]
        local = jnp.sum((kept_re * kept_re + kept_im * kept_im).reshape(-1, 8, piece // 128, 128), (0, 2))
        total = jnp.sum(sum_everywhere(8, strings, planes, local))
        rms = jnp.sqrt(total / count_all + EPS_NORM)
        new_re = (states[:, 0].astype(f32) + TAU_STEP * g_re / rms).astype(bf16)
        new_im = (states[:, 1].astype(f32) + TAU_STEP * g_im / rms).astype(bf16)
        chain = jnp.stack([new_re, new_im], 1)
    new_re, new_im = exchange(
        "collect", 9, strings, here, over_string, collect,
        (chain,), (shape((bands, width), bf16), shape((bands, width), bf16)), 2,
    )
    return (new_re[None], new_im[None])


def solution(mesh):
    placed = (P("kstr", None, "pw"), P("kstr", None, "pw"), P("pw"))
    strings, planes = mesh.shape["kstr"], mesh.shape["pw"]

    def body(states_re, states_im, gmap):
        kpoints, bands, width = states_re.shape
        fits = (
            kpoints == 1
            and strings > 1
            and planes > 1
            and width % (strings * 128) == 0
            and bands % (planes * 16) == 0
            and bands % 128 == 0
            and planes % 2 == 0
            and strings == 2 * STEPS
        )
        if not fits:
            return general_body(states_re, states_im, gmap)
        return spread_body(strings, planes, states_re, states_im, gmap)

    return jax.shard_map(
        body,
        mesh=mesh,
        in_specs=placed,
        out_specs=(P("kstr", None, "pw"), P("kstr", None, "pw")),
        check_vma=False,
    )
```

```python
import functools

import jax
import jax.numpy as jnp
from jax import lax
from jax.experimental import pallas as pl
from jax.experimental.pallas import tpu as pltpu
from jax.sharding import PartitionSpec as P

NEWTON = 4
STEPS = 2


HIGH = lax.Precision.HIGHEST
EPS_SCALE = 1e-06
EPS_NORM = 1e-06
TAU_STEP = 0.25


def shifted(value, axis, by):
    count = lax.axis_size(axis)
    return lax.ppermute(value, axis, [(i, (i + by) % count) for i in range(count)])


def padded_2(block, sides, width):
    for axis, dim in sides:
        count = lax.axis_size(axis)
        forward = [(i, i + 1) for i in range(count - 1)]
        forward.append((count - 1, 0))
        backward = [(target, source) for source, target in forward]
        low = lax.ppermute(
            lax.slice_in_dim(block, block.shape[dim] - width, None, axis=dim), axis, forward
        )
        high = lax.ppermute(lax.slice_in_dim(block, 0, width, axis=dim), axis, backward)
        block = jnp.concatenate([low, block, high], axis=dim)
    return block


def complex_mul(left, right):

    def matmul(first, second):
        return jnp.einsum("kij,kjl->kil", first, second, precision=HIGH)

    real = matmul(left[:, 0], right[:, 0]) - matmul(left[:, 1], right[:, 1])
    imag = matmul(left[:, 0], right[:, 1]) + matmul(left[:, 1], right[:, 0])
    return jnp.stack([real, imag], 1)


def start_inverse(whole):
    magnitude = jnp.sqrt(whole[:, 0] * whole[:, 0] + whole[:, 1] * whole[:, 1])
    colmax = jnp.max(jnp.sum(magnitude, axis=1), axis=1)
    rowmax = jnp.max(jnp.sum(magnitude, axis=2), axis=1)
    factor = (1.0 / (colmax * rowmax + EPS_SCALE))[:, None, None]
    return jnp.stack(
        [jnp.swapaxes(whole[:, 0], 1, 2) * factor, -jnp.swapaxes(whole[:, 1], 1, 2) * factor], 1
    )


def newton_full(whole):
    iterate = start_inverse(whole)
    for turn in range(NEWTON):
        iterate = 2.0 * iterate - complex_mul(iterate, complex_mul(whole, iterate))
    return iterate


def bf_product(form, left, right):
    return jnp.einsum(form, left, right, preferred_element_type=jnp.float32)


def dual_terms(rounded, states):
    real = bf_product("kmn,kmg->kng", rounded[:, 0], states[:, 0]) + bf_product(
        "kmn,kmg->kng", rounded[:, 1], states[:, 1]
    )
    imag = bf_product("kmn,kmg->kng", rounded[:, 0], states[:, 1]) - bf_product(
        "kmn,kmg->kng", rounded[:, 1], states[:, 0]
    )
    return jnp.stack([real, imag], 1).astype(jnp.bfloat16)


def rotate_columns(block, amount, width):
    blocks_off = amount // width
    rest = amount % width
    plane_size = lax.axis_size("pw")
    for bit in range((plane_size - 1).bit_length()):
        moved = shifted(block, "pw", -(1 << bit))
        block = jnp.where(jnp.bitwise_and(jnp.right_shift(blocks_off, bit), 1) == 1, moved, block)
    after = shifted(block, "pw", -1)
    joined = jnp.concatenate([block, after], block.ndim - 1)
    return lax.dynamic_slice_in_dim(joined, rest, width, block.ndim - 1)


def general_body(states_re, states_im, gmap):
    kpoints, bands, width = states_re.shape
    string_size = lax.axis_size("kstr")
    plane_size = lax.axis_size("pw")
    string_index = lax.axis_index("kstr")
    total_width = width * plane_size
    offset = jnp.mod(gmap[0] - lax.axis_index("pw") * width, total_width)
    back_offset = jnp.mod(total_width - offset, total_width)
    at_first = string_index == 0
    at_last = string_index == string_size - 1
    count_all = 2 * kpoints * string_size * bands * width * plane_size
    states = jnp.stack([states_re, states_im], 1)
    for step in range(STEPS):
        padded = padded_2(states, (("kstr", 0),), 1)
        ahead = padded[-1:]
        behind = padded[:1]
        turned = rotate_columns(ahead, offset, width)
        ahead = jnp.where(at_last, turned, ahead)
        following = jnp.concatenate([states[1:], ahead], 0)
        s_re = bf_product("kmg,kng->kmn", states[:, 0], following[:, 0]) + bf_product(
            "kmg,kng->kmn", states[:, 1], following[:, 1]
        )
        s_im = bf_product("kmg,kng->kmn", states[:, 0], following[:, 1]) - bf_product(
            "kmg,kng->kmn", states[:, 1], following[:, 0]
        )
        partial_value = jnp.stack([s_re, s_im], 1)
        whole = lax.psum(partial_value, "pw") / (width * plane_size)
        inverse = newton_full(whole)
        rounded = inverse.astype(jnp.bfloat16)
        a_re = bf_product("kmn,kmg->kng", rounded[:, 0], following[:, 0]) - bf_product(
            "kmn,kmg->kng", rounded[:, 1], following[:, 1]
        )
        a_im = bf_product("kmn,kmg->kng", rounded[:, 0], following[:, 1]) + bf_product(
            "kmn,kmg->kng", rounded[:, 1], following[:, 0]
        )
        earlier = dual_terms(rounded[:-1], states[:-1])
        previous_inverse = shifted(rounded, "kstr", 1)
        arrived = dual_terms(previous_inverse, behind)
        placed = rotate_columns(arrived, back_offset, width)
        arrived = jnp.where(at_first, placed, arrived)
        incoming = jnp.concatenate([arrived, earlier], 0).astype(jnp.float32)
        g_re = a_im - incoming[:, 1]
        g_im = incoming[:, 0] - a_re
        total = lax.psum(jnp.sum(g_re * g_re + g_im * g_im), ("kstr", "pw"))
        rms = jnp.sqrt(total / count_all + EPS_NORM)
        new_re = (states[:, 0].astype(jnp.float32) + TAU_STEP * g_re / rms).astype(jnp.bfloat16)
        new_im = (states[:, 1].astype(jnp.float32) + TAU_STEP * g_im / rms).astype(jnp.bfloat16)
        states = jnp.stack([new_re, new_im], 1)
    return (states[:, 0], states[:, 1])


def halves(value):
    high = value.astype(jnp.bfloat16)
    return high, (value - high.astype(jnp.float32)).astype(jnp.bfloat16)


def left_factor(real, imag):
    real_high, real_low = halves(real)
    imag_high, imag_low = halves(imag)
    high = jnp.concatenate([real_high, imag_high], 1)
    return jnp.concatenate([high, high, real_low, imag_low], 1)


def right_factor(real, imag):
    real_high, real_low = halves(real)
    imag_high, imag_low = halves(imag)
    high = [
        jnp.concatenate([real_high, imag_high], 1),
        jnp.concatenate([-imag_high, real_high], 1),
    ]
    low = [
        jnp.concatenate([real_low, imag_low], 1),
        jnp.concatenate([-imag_low, real_low], 1),
    ]
    return jnp.concatenate(high + low + high, 0)


def newton_turned(real, imag):
    bands = real.shape[0]
    magnitude = jnp.sqrt(real * real + imag * imag)
    colmax = jnp.max(jnp.sum(magnitude, axis=0, keepdims=True), axis=1, keepdims=True)
    rowmax = jnp.max(jnp.sum(magnitude, axis=1, keepdims=True), axis=0, keepdims=True)
    factor = 1.0 / (colmax * rowmax + EPS_SCALE)
    x_re, x_im = real.T * factor, -imag.T * factor
    whole = left_factor(real, imag)
    for turn in range(NEWTON):
        p = jnp.dot(whole, right_factor(x_re, x_im), preferred_element_type=jnp.float32)
        q = jnp.dot(
            left_factor(x_re, x_im),
            right_factor(p[:, :bands], p[:, bands:]),
            preferred_element_type=jnp.float32,
        )
        x_re = 2.0 * x_re - q[:, :bands]
        x_im = 2.0 * x_im - q[:, bands:]
    return x_re.T.astype(jnp.bfloat16), x_im.T.astype(jnp.bfloat16)


def remote_copy(source, place, send, recv, target):
    return pltpu.make_async_remote_copy(
        src_ref=source,
        dst_ref=place,
        send_sem=send,
        recv_sem=recv,
        device_id=target,
        device_id_type=pl.DeviceIdType.MESH,
    )


def greet_all(greeted, awaited):
    barrier = pltpu.get_barrier_semaphore()
    for peer in greeted:
        pl.semaphore_signal(barrier, inc=1, device_id=peer, device_id_type=pl.DeviceIdType.MESH)
    pl.semaphore_wait(barrier, awaited)


def spread(strings, planes, states_re, states_im):
    bands, width = states_re.shape
    piece = width // strings

    def kernel(re_ref, im_ref, out_ref, joined_ref, send, recv, local):
        k, p = lax.axis_index("kstr"), lax.axis_index("pw")
        forward = (k < STEPS).astype(jnp.int32)
        giver = (k, lax.rem(p + planes - 1 + 2 * forward, planes))
        taker = (k, lax.rem(p + planes + 1 - 2 * forward, planes))
        string_peers = [(lax.rem(k + step, strings), p) for step in range(1, strings)]
        greet_all(string_peers + [giver], strings)
        kept = pl.ds(pl.multiple_of((1 - forward) * width, width), width)
        other = pl.ds(pl.multiple_of(forward * width, width), width)
        mine = pl.ds(pl.multiple_of(k * piece, piece), piece)
        copies, inside = [], []
        for part, ref in enumerate((re_ref, im_ref)):
            for slot, peer in enumerate(string_peers):
                cut = pl.ds(pl.multiple_of(peer[0] * piece, piece), piece)
                copies.append(
                    remote_copy(
                        ref.at[:, cut], out_ref.at[k, part], send.at[slot, part], recv.at[slot, part], peer
                    )
                )
            slot = strings - 1
            copies.append(
                remote_copy(
                    ref, joined_ref.at[part, :, other], send.at[slot, part], recv.at[slot, part], taker
                )
            )
            inside.append(
                pltpu.make_async_copy(ref, joined_ref.at[part, :, kept], local.at[0, part])
            )
            inside.append(
                pltpu.make_async_copy(ref.at[:, mine], out_ref.at[k, part], local.at[1, part])
            )
        for copy in copies + inside:
            copy.start()
        for copy in inside + copies:
            copy.wait()

    vmem = pl.BlockSpec(memory_space=pltpu.VMEM)
    return pl.pallas_call(
        kernel,
        out_shape=(
            jax.ShapeDtypeStruct((strings, 2, bands, piece), states_re.dtype),
            jax.ShapeDtypeStruct((2, bands, 2 * width), states_re.dtype),
        ),
        in_specs=[vmem, vmem],
        out_specs=(vmem, vmem),
        scratch_shapes=[
            pltpu.SemaphoreType.DMA((strings, 2)),
            pltpu.SemaphoreType.DMA((strings, 2)),
            pltpu.SemaphoreType.DMA((2, 2)),
        ],
        compiler_params=pltpu.CompilerParams(collective_id=1, has_side_effects=True),
        name="spread",
    )(states_re, states_im)


def turn_blocks(strings, planes, shift, aligned):
    _, bands, width = aligned.shape
    piece = width // strings

    def kernel(block_ref, out_ref, send, recv, local):
        k, p = lax.axis_index("kstr"), lax.axis_index("pw")
        up, down = lax.rem(p + shift, planes), lax.rem(p + planes - shift, planes)
        steps = range(1 if shift == 0 else 0, strings)
        forward = (k < STEPS).astype(jnp.int32)
        target_plane = forward * down + (1 - forward) * up
        givers, takers = [], []
        for step in steps:
            other = lax.rem(k + strings - step, strings)
            ahead = (other < STEPS).astype(jnp.int32)
            givers.append((other, ahead * up + (1 - ahead) * down))
            takers.append((lax.rem(k + step, strings), target_plane))
        greet_all(givers, len(takers))
        copies = []
        for slot, taker in enumerate(takers):
            cut = pl.ds(pl.multiple_of(taker[0] * piece, piece), piece)
            copies.append(
                remote_copy(
                    block_ref.at[:, :, cut], out_ref.at[k], send.at[slot], recv.at[slot], taker
                )
            )
        for copy in copies:
            copy.start()
        if shift == 0:
            cut = pl.ds(pl.multiple_of(k * piece, piece), piece)
            inside = pltpu.make_async_copy(block_ref.at[:, :, cut], out_ref.at[k], local.at[0])
            inside.start()
            inside.wait()
        for copy in copies:
            copy.wait()

    vmem = pl.BlockSpec(memory_space=pltpu.VMEM)
    return pl.pallas_call(
        kernel,
        out_shape=jax.ShapeDtypeStruct((strings, 2, bands, piece), aligned.dtype),
        in_specs=[vmem],
        out_specs=vmem,
        scratch_shapes=[
            pltpu.SemaphoreType.DMA((strings,)),
            pltpu.SemaphoreType.DMA((strings,)),
            pltpu.SemaphoreType.DMA((1,)),
        ],
        compiler_params=pltpu.CompilerParams(collective_id=20 + shift, has_side_effects=True),
        name=f"turn_{shift}",
    )(aligned)


def margin_of(own, ahead):
    left = jnp.concatenate([own[0], own[1]], 1)
    form = (((1,), (1,)), ((), ()))
    real = lax.dot_general(
        left, jnp.concatenate([ahead[0], ahead[1]], 1), form, preferred_element_type=jnp.float32
    )
    imag = lax.dot_general(
        left, jnp.concatenate([ahead[1], -ahead[0]], 1), form, preferred_element_type=jnp.float32
    )
    return real, imag


def both_steps(strings, planes, states, halo):
    _, _, bands, piece = states.shape
    total_width = piece * strings * planes
    count_all = 2 * strings * bands * total_width
    share, middle = bands // planes, bands // 2
    chunks = bands // 128
    bf16, f32 = jnp.bfloat16, jnp.float32

    def kernel(states_ref, halo_ref, re_ref, im_ref, *scratch):
        chains, scratch = scratch[: STEPS + 1], scratch[STEPS + 1 :]
        part, got_string, summed, got_planes, block, whole, rounded, inverse = scratch[:8]
        grad, tile, first, stage, second, load, kept = scratch[8:15]
        send1, recv1, send2, recv2, send3, recv3, send4, recv4, send5, recv5 = scratch[15:25]
        send6, recv6, send7, recv7, send8, recv8 = scratch[25:]
        k, p = lax.axis_index("kstr"), lax.axis_index("pw")
        string_peers = [(lax.rem(k + step, strings), p) for step in range(1, strings)]
        plane_peers = [(k, lax.rem(p + step, planes)) for step in range(1, planes)]
        side = lax.rem(p, 2)
        sibling = (k, p + 1 - 2 * side)

        def rows(index, size):
            return pl.ds(pl.multiple_of(index * size, size), size)

        barrier = pltpu.get_barrier_semaphore()
        for peer in string_peers + plane_peers:
            pl.semaphore_signal(
                barrier, inc=1, device_id=peer, device_id_type=pl.DeviceIdType.MESH
            )

        loads = [
            pltpu.make_async_copy(
                halo_ref.at[strings - STEPS :], chains[0].at[:STEPS], load.at[0]
            ),
            pltpu.make_async_copy(states_ref, chains[0].at[STEPS : STEPS + strings], load.at[1]),
            pltpu.make_async_copy(
                halo_ref.at[:STEPS], chains[0].at[STEPS + strings :], load.at[2]
            ),
        ]
        for copy in loads:
            copy.start()
        for copy in loads:
            copy.wait()
        cuts = [pl.ds(chunk * 128, 128) for chunk in range(chunks)]

        def put_margin(chain_ref, wide, slot, which):
            real, imag = margin_of(chain_ref[wide + 1 + which], chain_ref[wide + 2 + which])
            part[slot, 0] = (real * (1.0 / total_width)).astype(bf16)
            part[slot, 1] = (imag * (1.0 / total_width)).astype(bf16)

        def find_inverses(chain_ref, wide, opening):
            over_string = []
            for slot, peer in enumerate(string_peers):
                put_margin(chain_ref, wide, slot, peer[0])
                if opening and slot == 0:
                    pl.semaphore_wait(barrier, len(string_peers) + len(plane_peers))
                for chunk, cut in enumerate(cuts):
                    copy = remote_copy(
                        part.at[slot, :, :, cut], got_string.at[slot, :, :, cut],
                        send1.at[slot, chunk], recv1.at[slot, chunk], peer,
                    )
                    copy.start()
                    over_string.append((chunk, copy))
            put_margin(chain_ref, wide, strings - 1, k)

            over_planes = []
            for chunk, cut in enumerate(cuts):
                for number, copy in over_string:
                    if number == chunk:
                        copy.wait()
                total = part[strings - 1, :, :, cut].astype(f32)
                for slot in range(strings - 1):
                    total = total + got_string[slot, :, :, cut].astype(f32)
                summed[:, :, cut] = total.astype(bf16)
                for slot, peer in enumerate(plane_peers):
                    copy = remote_copy(
                        summed.at[:, rows(peer[1], share), cut], got_planes.at[slot, :, :, cut],
                        send2.at[slot, chunk], recv2.at[slot, chunk], peer,
                    )
                    copy.start()
                    over_planes.append((chunk, copy))
            back = []
            for chunk, cut in enumerate(cuts):
                for number, copy in over_planes:
                    if number == chunk:
                        copy.wait()
                total = summed[:, rows(p, share), cut].astype(f32)
                for slot in range(planes - 1):
                    total = total + got_planes[slot, :, :, cut].astype(f32)
                block[:, :, cut] = total.astype(bf16)
                for slot, peer in enumerate(plane_peers):
                    copy = remote_copy(
                        block.at[:, :, cut], whole.at[:, rows(p, share), cut],
                        send3.at[slot, chunk], recv3.at[slot, chunk], peer,
                    )
                    copy.start()
                    back.append(copy)
                whole[:, rows(p, share), cut] = block[:, :, cut]
            for copy in back:
                copy.wait()

            real, imag = newton_turned(whole[0].astype(f32), whole[1].astype(f32))
            rounded[0] = real
            rounded[1] = imag
            mine = rows(side, middle)
            first = []
            for slot, peer in enumerate(string_peers):
                copy = remote_copy(
                    rounded.at[:, mine, :], inverse.at[k, :, mine, :],
                    send4.at[slot], recv4.at[slot], peer,
                )
                copy.start()
                first.append(copy)
            inverse[k, 0] = real
            inverse[k, 1] = imag
            second = []
            for slot, copy in enumerate(first):
                copy.wait()
                source = lax.rem(k + strings - slot - 1, strings)
                relay = remote_copy(
                    inverse.at[source, :, mine, :], inverse.at[source, :, mine, :],
                    send5.at[slot], recv5.at[slot], sibling,
                )
                relay.start()
                second.append(relay)
            for relay in second:
                relay.wait()

        def find_gradient(chain_ref, wide):
            def element(index, total):
                link = lax.rem(index + strings - wide, strings)
                before = lax.rem(index + strings - wide - 1, strings)

                def product(left, right):
                    return jnp.dot(left, right, preferred_element_type=f32)

                x_re, x_im = inverse[link, 0], inverse[link, 1]
                next_re, next_im = chain_ref[index + 2, 0], chain_ref[index + 2, 1]
                a_re = product(x_re, next_re) - product(x_im, next_im)
                a_im = product(x_re, next_im) + product(x_im, next_re)
                x_re, x_im = inverse[before, 0], inverse[before, 1]
                last_re, last_im = chain_ref[index, 0], chain_ref[index, 1]
                c_re = (product(x_re, last_re) + product(x_im, last_im)).astype(bf16)
                c_im = (product(x_re, last_im) - product(x_im, last_re)).astype(bf16)
                g_re = a_im - c_im.astype(f32)
                g_im = c_re.astype(f32) - a_re
                grad[index, 0] = g_re
                grad[index, 1] = g_im
                square = g_re * g_re + g_im * g_im
                lanes = square[:, :128]
                for group in range(1, piece // 128):
                    lanes = lanes + square[:, group * 128 : (group + 1) * 128]
                sums = jnp.sum(lanes.reshape(bands // 8, 8, 128), 0)
                inside = jnp.logical_and(index >= wide, index < wide + strings)
                return total + jnp.where(inside, sums, jnp.zeros_like(sums))

            tile[...] = lax.fori_loop(
                0, strings + 2 * wide, element, jnp.zeros((8, 128), f32)
            )
            copies = [
                remote_copy(tile, first.at[k], send6.at[slot], recv6.at[slot], peer)
                for slot, peer in enumerate(string_peers)
            ]
            for copy in copies:
                copy.start()
            first[k] = tile[...]
            for copy in copies:
                copy.wait()
            stage[...] = jnp.sum(first[...], 0)
            copies = [
                remote_copy(stage, second.at[p], send7.at[slot], recv7.at[slot], peer)
                for slot, peer in enumerate(plane_peers)
            ]
            for copy in copies:
                copy.start()
            second[p] = stage[...]
            for copy in copies:
                copy.wait()
            total = jnp.sum(second[...], 0)
            total = jnp.sum(jnp.sum(total, axis=0, keepdims=True), axis=1, keepdims=True)
            return TAU_STEP / jnp.sqrt(total / count_all + EPS_NORM)

        def renewed(chain_ref, index, part_index, scale):
            old = chain_ref[index + 1, part_index].astype(f32)
            return (old + grad[index, part_index] * scale).astype(bf16)

        def renew(chain_ref, next_ref, count, scale):
            def element(index, carry):
                next_ref[index, 0] = renewed(chain_ref, index, 0, scale)
                next_ref[index, 1] = renewed(chain_ref, index, 1, scale)
                return carry

            lax.fori_loop(0, count, element, 0)

        def finish(chain_ref, next_ref, scale):
            copies = []
            mine = rows(k, piece)
            for slot, peer in enumerate(string_peers):
                for index, ref in enumerate((re_ref, im_ref)):
                    next_ref[slot, index] = renewed(chain_ref, peer[0], index, scale)
                    copy = remote_copy(
                        next_ref.at[slot, index], ref.at[:, mine],
                        send8.at[slot, index], recv8.at[slot, index], peer,
                    )
                    copy.start()
                    copies.append(copy)
            for index, ref in enumerate((re_ref, im_ref)):
                next_ref[strings - 1, index] = renewed(chain_ref, k, index, scale)
                copy = pltpu.make_async_copy(
                    next_ref.at[strings - 1, index], ref.at[:, mine], kept.at[index]
                )
                copy.start()
                copies.append(copy)
            for copy in copies:
                copy.wait()

        for turn in range(STEPS):
            wide = STEPS - 1 - turn
            find_inverses(chains[turn], wide, turn == 0)
            scale = find_gradient(chains[turn], wide)
            if wide > 0:
                renew(chains[turn], chains[turn + 1], strings + 2 * wide, scale)
        finish(chains[STEPS - 1], chains[STEPS], scale)

    vmem = pl.BlockSpec(memory_space=pltpu.VMEM)
    anywhere = pl.BlockSpec(memory_space=pl.ANY)
    square = (2, bands, bands)
    dma = pltpu.SemaphoreType.DMA
    lengths = [strings + 2 * (STEPS - step) for step in range(STEPS + 1)]
    out = jax.ShapeDtypeStruct((bands, piece * strings), bf16)
    return pl.pallas_call(
        kernel,
        out_shape=(out, out),
        in_specs=[anywhere, anywhere],
        out_specs=(vmem, vmem),
        scratch_shapes=[pltpu.VMEM((length, 2, bands, piece), bf16) for length in lengths]
        + [
            pltpu.VMEM((strings,) + square, bf16),
            pltpu.VMEM((strings - 1,) + square, bf16),
            pltpu.VMEM(square, bf16),
            pltpu.VMEM((planes - 1, 2, share, bands), bf16),
            pltpu.VMEM((2, share, bands), bf16),
            pltpu.VMEM(square, bf16),
            pltpu.VMEM(square, bf16),
            pltpu.VMEM((strings,) + square, bf16),
            pltpu.VMEM((lengths[1], 2, bands, piece), f32),
            pltpu.VMEM((8, 128), f32),
            pltpu.VMEM((strings, 8, 128), f32),
            pltpu.VMEM((8, 128), f32),
            pltpu.VMEM((planes, 8, 128), f32),
            dma((3,)),
            dma((2,)),
        ]
        + [dma((strings - 1, chunks))] * 2
        + [dma((planes - 1, chunks))] * 4
        + [dma((strings - 1,))] * 4
        + [dma((strings - 1,))] * 2
        + [dma((planes - 1,))] * 2
        + [dma((strings - 1, 2))] * 2,
        compiler_params=pltpu.CompilerParams(collective_id=4, has_side_effects=True),
        name="both_steps",
    )(states, halo)


def spread_body(strings, planes, states_re, states_im, gmap):
    width = states_re.shape[2]
    total_width = width * planes
    offset = jnp.mod(gmap[0] - lax.axis_index("pw") * width, total_width)
    states, joined = spread(strings, planes, states_re[0], states_im[0])
    blocks_off, rest = offset // width, jnp.mod(offset, width)
    start = jnp.where(lax.axis_index("kstr") < STEPS, rest, width - rest)
    aligned = lax.dynamic_slice_in_dim(joined, start, width, 2)
    halo = lax.switch(
        blocks_off,
        [functools.partial(turn_blocks, strings, planes, shift) for shift in range(planes)],
        aligned,
    )
    new_re, new_im = both_steps(strings, planes, states, halo)
    return (new_re[None], new_im[None])


def solution(mesh):
    placed = (P("kstr", None, "pw"), P("kstr", None, "pw"), P("pw"))
    strings, planes = mesh.shape["kstr"], mesh.shape["pw"]

    def body(states_re, states_im, gmap):
        kpoints, bands, width = states_re.shape
        fits = (
            kpoints == 1
            and strings > 1
            and planes > 1
            and width % (strings * 128) == 0
            and bands % (planes * 16) == 0
            and bands % 128 == 0
            and planes % 2 == 0
            and strings == 2 * STEPS
        )
        if not fits:
            return general_body(states_re, states_im, gmap)
        return spread_body(strings, planes, states_re, states_im, gmap)

    return jax.shard_map(
        body,
        mesh=mesh,
        in_specs=placed,
        out_specs=(P("kstr", None, "pw"), P("kstr", None, "pw")),
        check_vma=False,
    )
```

```python
import functools

import jax
import jax.numpy as jnp
from jax import lax
from jax.experimental import pallas as pl
from jax.experimental.pallas import tpu as pltpu
from jax.sharding import PartitionSpec as P

NEWTON = 4
STEPS = 2


HIGH = lax.Precision.HIGHEST
EPS_SCALE = 1e-06
EPS_NORM = 1e-06
TAU_STEP = 0.25


def shifted(value, axis, by):
    count = lax.axis_size(axis)
    return lax.ppermute(value, axis, [(i, (i + by) % count) for i in range(count)])


def padded_2(block, sides, width):
    for axis, dim in sides:
        count = lax.axis_size(axis)
        forward = [(i, i + 1) for i in range(count - 1)]
        forward.append((count - 1, 0))
        backward = [(target, source) for source, target in forward]
        low = lax.ppermute(
            lax.slice_in_dim(block, block.shape[dim] - width, None, axis=dim), axis, forward
        )
        high = lax.ppermute(lax.slice_in_dim(block, 0, width, axis=dim), axis, backward)
        block = jnp.concatenate([low, block, high], axis=dim)
    return block


def complex_mul(left, right):

    def matmul(first, second):
        return jnp.einsum("kij,kjl->kil", first, second, precision=HIGH)

    real = matmul(left[:, 0], right[:, 0]) - matmul(left[:, 1], right[:, 1])
    imag = matmul(left[:, 0], right[:, 1]) + matmul(left[:, 1], right[:, 0])
    return jnp.stack([real, imag], 1)


def start_inverse(whole):
    magnitude = jnp.sqrt(whole[:, 0] * whole[:, 0] + whole[:, 1] * whole[:, 1])
    colmax = jnp.max(jnp.sum(magnitude, axis=1), axis=1)
    rowmax = jnp.max(jnp.sum(magnitude, axis=2), axis=1)
    factor = (1.0 / (colmax * rowmax + EPS_SCALE))[:, None, None]
    return jnp.stack(
        [jnp.swapaxes(whole[:, 0], 1, 2) * factor, -jnp.swapaxes(whole[:, 1], 1, 2) * factor], 1
    )


def newton_full(whole):
    iterate = start_inverse(whole)
    for turn in range(NEWTON):
        iterate = 2.0 * iterate - complex_mul(iterate, complex_mul(whole, iterate))
    return iterate


def bf_product(form, left, right):
    return jnp.einsum(form, left, right, preferred_element_type=jnp.float32)


def dual_terms(rounded, states):
    real = bf_product("kmn,kmg->kng", rounded[:, 0], states[:, 0]) + bf_product(
        "kmn,kmg->kng", rounded[:, 1], states[:, 1]
    )
    imag = bf_product("kmn,kmg->kng", rounded[:, 0], states[:, 1]) - bf_product(
        "kmn,kmg->kng", rounded[:, 1], states[:, 0]
    )
    return jnp.stack([real, imag], 1).astype(jnp.bfloat16)


def rotate_columns(block, amount, width):
    blocks_off = amount // width
    rest = amount % width
    plane_size = lax.axis_size("pw")
    for bit in range((plane_size - 1).bit_length()):
        moved = shifted(block, "pw", -(1 << bit))
        block = jnp.where(jnp.bitwise_and(jnp.right_shift(blocks_off, bit), 1) == 1, moved, block)
    after = shifted(block, "pw", -1)
    joined = jnp.concatenate([block, after], block.ndim - 1)
    return lax.dynamic_slice_in_dim(joined, rest, width, block.ndim - 1)


def general_body(states_re, states_im, gmap):
    kpoints, bands, width = states_re.shape
    string_size = lax.axis_size("kstr")
    plane_size = lax.axis_size("pw")
    string_index = lax.axis_index("kstr")
    total_width = width * plane_size
    offset = jnp.mod(gmap[0] - lax.axis_index("pw") * width, total_width)
    back_offset = jnp.mod(total_width - offset, total_width)
    at_first = string_index == 0
    at_last = string_index == string_size - 1
    count_all = 2 * kpoints * string_size * bands * width * plane_size
    states = jnp.stack([states_re, states_im], 1)
    for step in range(STEPS):
        padded = padded_2(states, (("kstr", 0),), 1)
        ahead = padded[-1:]
        behind = padded[:1]
        turned = rotate_columns(ahead, offset, width)
        ahead = jnp.where(at_last, turned, ahead)
        following = jnp.concatenate([states[1:], ahead], 0)
        s_re = bf_product("kmg,kng->kmn", states[:, 0], following[:, 0]) + bf_product(
            "kmg,kng->kmn", states[:, 1], following[:, 1]
        )
        s_im = bf_product("kmg,kng->kmn", states[:, 0], following[:, 1]) - bf_product(
            "kmg,kng->kmn", states[:, 1], following[:, 0]
        )
        partial_value = jnp.stack([s_re, s_im], 1)
        whole = lax.psum(partial_value, "pw") / (width * plane_size)
        inverse = newton_full(whole)
        rounded = inverse.astype(jnp.bfloat16)
        a_re = bf_product("kmn,kmg->kng", rounded[:, 0], following[:, 0]) - bf_product(
            "kmn,kmg->kng", rounded[:, 1], following[:, 1]
        )
        a_im = bf_product("kmn,kmg->kng", rounded[:, 0], following[:, 1]) + bf_product(
            "kmn,kmg->kng", rounded[:, 1], following[:, 0]
        )
        earlier = dual_terms(rounded[:-1], states[:-1])
        previous_inverse = shifted(rounded, "kstr", 1)
        arrived = dual_terms(previous_inverse, behind)
        placed = rotate_columns(arrived, back_offset, width)
        arrived = jnp.where(at_first, placed, arrived)
        incoming = jnp.concatenate([arrived, earlier], 0).astype(jnp.float32)
        g_re = a_im - incoming[:, 1]
        g_im = incoming[:, 0] - a_re
        total = lax.psum(jnp.sum(g_re * g_re + g_im * g_im), ("kstr", "pw"))
        rms = jnp.sqrt(total / count_all + EPS_NORM)
        new_re = (states[:, 0].astype(jnp.float32) + TAU_STEP * g_re / rms).astype(jnp.bfloat16)
        new_im = (states[:, 1].astype(jnp.float32) + TAU_STEP * g_im / rms).astype(jnp.bfloat16)
        states = jnp.stack([new_re, new_im], 1)
    return (states[:, 0], states[:, 1])


def halves(value):
    high = value.astype(jnp.bfloat16)
    return high, (value - high.astype(jnp.float32)).astype(jnp.bfloat16)


def left_factor(real, imag):
    real_high, real_low = halves(real)
    imag_high, imag_low = halves(imag)
    high = jnp.concatenate([real_high, imag_high], 1)
    return jnp.concatenate([high, high, real_low, imag_low], 1)


def right_factor(real, imag):
    real_high, real_low = halves(real)
    imag_high, imag_low = halves(imag)
    high = [
        jnp.concatenate([real_high, imag_high], 1),
        jnp.concatenate([-imag_high, real_high], 1),
    ]
    low = [
        jnp.concatenate([real_low, imag_low], 1),
        jnp.concatenate([-imag_low, real_low], 1),
    ]
    return jnp.concatenate(high + low + high, 0)


def newton_turned(real, imag):
    bands = real.shape[0]
    magnitude = jnp.sqrt(real * real + imag * imag)
    colmax = jnp.max(jnp.sum(magnitude, axis=0, keepdims=True), axis=1, keepdims=True)
    rowmax = jnp.max(jnp.sum(magnitude, axis=1, keepdims=True), axis=0, keepdims=True)
    factor = 1.0 / (colmax * rowmax + EPS_SCALE)
    x_re, x_im = real.T * factor, -imag.T * factor
    whole = left_factor(real, imag)
    for turn in range(NEWTON):
        p = jnp.dot(whole, right_factor(x_re, x_im), preferred_element_type=jnp.float32)
        q = jnp.dot(
            left_factor(x_re, x_im),
            right_factor(p[:, :bands], p[:, bands:]),
            preferred_element_type=jnp.float32,
        )
        x_re = 2.0 * x_re - q[:, :bands]
        x_im = 2.0 * x_im - q[:, bands:]
    return x_re.T.astype(jnp.bfloat16), x_im.T.astype(jnp.bfloat16)


def remote_copy(source, place, send, recv, target):
    return pltpu.make_async_remote_copy(
        src_ref=source,
        dst_ref=place,
        send_sem=send,
        recv_sem=recv,
        device_id=target,
        device_id_type=pl.DeviceIdType.MESH,
    )


def greet_all(greeted, awaited):
    barrier = pltpu.get_barrier_semaphore()
    for peer in greeted:
        pl.semaphore_signal(barrier, inc=1, device_id=peer, device_id_type=pl.DeviceIdType.MESH)
    pl.semaphore_wait(barrier, awaited)


def spread(strings, planes, states_re, states_im):
    bands, width = states_re.shape
    piece = width // strings

    def kernel(re_ref, im_ref, out_ref, joined_ref, send, recv, local):
        k, p = lax.axis_index("kstr"), lax.axis_index("pw")
        forward = (k < STEPS).astype(jnp.int32)
        giver = (k, lax.rem(p + planes - 1 + 2 * forward, planes))
        taker = (k, lax.rem(p + planes + 1 - 2 * forward, planes))
        string_peers = [(lax.rem(k + step, strings), p) for step in range(1, strings)]
        greet_all(string_peers + [giver], strings)
        kept = pl.ds(pl.multiple_of((1 - forward) * width, width), width)
        other = pl.ds(pl.multiple_of(forward * width, width), width)
        mine = pl.ds(pl.multiple_of(k * piece, piece), piece)
        copies, inside = [], []
        for part, ref in enumerate((re_ref, im_ref)):
            for slot, peer in enumerate(string_peers):
                cut = pl.ds(pl.multiple_of(peer[0] * piece, piece), piece)
                copies.append(
                    remote_copy(
                        ref.at[:, cut], out_ref.at[k, part], send.at[slot, part], recv.at[slot, part], peer
                    )
                )
            slot = strings - 1
            copies.append(
                remote_copy(
                    ref, joined_ref.at[part, :, other], send.at[slot, part], recv.at[slot, part], taker
                )
            )
            inside.append(
                pltpu.make_async_copy(ref, joined_ref.at[part, :, kept], local.at[0, part])
            )
            inside.append(
                pltpu.make_async_copy(ref.at[:, mine], out_ref.at[k, part], local.at[1, part])
            )
        for copy in copies + inside:
            copy.start()
        for copy in inside + copies:
            copy.wait()

    vmem = pl.BlockSpec(memory_space=pltpu.VMEM)
    return pl.pallas_call(
        kernel,
        out_shape=(
            jax.ShapeDtypeStruct((strings, 2, bands, piece), states_re.dtype),
            jax.ShapeDtypeStruct((2, bands, 2 * width), states_re.dtype),
        ),
        in_specs=[vmem, vmem],
        out_specs=(vmem, vmem),
        scratch_shapes=[
            pltpu.SemaphoreType.DMA((strings, 2)),
            pltpu.SemaphoreType.DMA((strings, 2)),
            pltpu.SemaphoreType.DMA((2, 2)),
        ],
        compiler_params=pltpu.CompilerParams(collective_id=1, has_side_effects=True),
        name="spread",
    )(states_re, states_im)


def turn_blocks(strings, planes, shift, aligned):
    _, bands, width = aligned.shape
    piece = width // strings

    def kernel(block_ref, out_ref, send, recv, local):
        k, p = lax.axis_index("kstr"), lax.axis_index("pw")
        up, down = lax.rem(p + shift, planes), lax.rem(p + planes - shift, planes)
        steps = range(1 if shift == 0 else 0, strings)
        forward = (k < STEPS).astype(jnp.int32)
        target_plane = forward * down + (1 - forward) * up
        givers, takers = [], []
        for step in steps:
            other = lax.rem(k + strings - step, strings)
            ahead = (other < STEPS).astype(jnp.int32)
            givers.append((other, ahead * up + (1 - ahead) * down))
            takers.append((lax.rem(k + step, strings), target_plane))
        greet_all(givers, len(takers))
        copies = []
        for slot, taker in enumerate(takers):
            cut = pl.ds(pl.multiple_of(taker[0] * piece, piece), piece)
            copies.append(
                remote_copy(
                    block_ref.at[:, :, cut], out_ref.at[k], send.at[slot], recv.at[slot], taker
                )
            )
        for copy in copies:
            copy.start()
        if shift == 0:
            cut = pl.ds(pl.multiple_of(k * piece, piece), piece)
            inside = pltpu.make_async_copy(block_ref.at[:, :, cut], out_ref.at[k], local.at[0])
            inside.start()
            inside.wait()
        for copy in copies:
            copy.wait()

    vmem = pl.BlockSpec(memory_space=pltpu.VMEM)
    return pl.pallas_call(
        kernel,
        out_shape=jax.ShapeDtypeStruct((strings, 2, bands, piece), aligned.dtype),
        in_specs=[vmem],
        out_specs=vmem,
        scratch_shapes=[
            pltpu.SemaphoreType.DMA((strings,)),
            pltpu.SemaphoreType.DMA((strings,)),
            pltpu.SemaphoreType.DMA((1,)),
        ],
        compiler_params=pltpu.CompilerParams(collective_id=20 + shift, has_side_effects=True),
        name=f"turn_{shift}",
    )(aligned)


def margin_of(own, ahead):
    left = jnp.concatenate([own[0], own[1]], 1)
    form = (((1,), (1,)), ((), ()))
    real = lax.dot_general(
        left, jnp.concatenate([ahead[0], ahead[1]], 1), form, preferred_element_type=jnp.float32
    )
    imag = lax.dot_general(
        left, jnp.concatenate([ahead[1], -ahead[0]], 1), form, preferred_element_type=jnp.float32
    )
    return real, imag


def both_steps(strings, planes, states, halo):
    _, _, bands, piece = states.shape
    total_width = piece * strings * planes
    count_all = 2 * strings * bands * total_width
    share, middle, pairs = bands // planes, bands // 2, planes // 2
    chunks = bands // 128
    bf16, f32 = jnp.bfloat16, jnp.float32

    def kernel(states_ref, halo_ref, re_ref, im_ref, *scratch):
        chains, scratch = scratch[: STEPS + 1], scratch[STEPS + 1 :]
        part, got_string, summed, got_planes, block, whole, rounded, inverse = scratch[:8]
        got_pair, half, scratch = scratch[8], scratch[9], scratch[:8] + scratch[10:]
        grad, tile, first, stage, second, load, kept = scratch[8:15]
        send1, recv1, send2, recv2, send3, recv3, send4, recv4, send5, recv5 = scratch[15:25]
        send6, recv6, send7, recv7, send8, recv8 = scratch[25:31]
        send0, recv0, send9, recv9 = scratch[31:]
        k, p = lax.axis_index("kstr"), lax.axis_index("pw")
        string_peers = [(lax.rem(k + step, strings), p) for step in range(1, strings)]
        plane_peers = [(k, lax.rem(p + step, planes)) for step in range(1, planes)]
        far_peers = [(k, lax.rem(p + 2 * step, planes)) for step in range(1, pairs)]
        side = lax.rem(p, 2)
        sibling = (k, p + 1 - 2 * side)

        def rows(index, size):
            return pl.ds(pl.multiple_of(index * size, size), size)

        barrier = pltpu.get_barrier_semaphore()
        for peer in string_peers + plane_peers:
            pl.semaphore_signal(
                barrier, inc=1, device_id=peer, device_id_type=pl.DeviceIdType.MESH
            )

        loads = [
            pltpu.make_async_copy(
                halo_ref.at[strings - STEPS :], chains[0].at[:STEPS], load.at[0]
            ),
            pltpu.make_async_copy(states_ref, chains[0].at[STEPS : STEPS + strings], load.at[1]),
            pltpu.make_async_copy(
                halo_ref.at[:STEPS], chains[0].at[STEPS + strings :], load.at[2]
            ),
        ]
        for copy in loads:
            copy.start()
        for copy in loads:
            copy.wait()
        cuts = [pl.ds(chunk * 128, 128) for chunk in range(chunks)]

        def put_margin(chain_ref, wide, slot, which):
            real, imag = margin_of(chain_ref[wide + 1 + which], chain_ref[wide + 2 + which])
            part[slot, 0] = (real * (1.0 / total_width)).astype(bf16)
            part[slot, 1] = (imag * (1.0 / total_width)).astype(bf16)

        def find_inverses(chain_ref, wide, opening):
            pair, over_string = [], []

            def carry_on(slot):
                pair[slot].wait()
                both = part[slot, :, rows(side, middle), :].astype(f32)
                half[slot] = (both + got_pair[slot].astype(f32)).astype(bf16)
                if slot == strings - 1:
                    return
                for chunk, cut in enumerate(cuts):
                    copy = remote_copy(
                        half.at[slot, :, :, cut], got_string.at[slot, :, :, cut],
                        send1.at[slot, chunk], recv1.at[slot, chunk], string_peers[slot],
                    )
                    copy.start()
                    over_string.append((chunk, copy))

            for slot in range(strings):
                which = k if slot == strings - 1 else string_peers[slot][0]
                put_margin(chain_ref, wide, slot, which)
                if opening and slot == 0:
                    pl.semaphore_wait(barrier, len(string_peers) + len(plane_peers))
                copy = remote_copy(
                    part.at[slot, :, rows(1 - side, middle), :], got_pair.at[slot],
                    send0.at[slot], recv0.at[slot], sibling,
                )
                copy.start()
                pair.append(copy)
                if slot > 0:
                    carry_on(slot - 1)
            carry_on(strings - 1)

            over_planes = []
            for chunk, cut in enumerate(cuts):
                for number, copy in over_string:
                    if number == chunk:
                        copy.wait()
                total = half[strings - 1, :, :, cut].astype(f32)
                for slot in range(strings - 1):
                    total = total + got_string[slot, :, :, cut].astype(f32)
                summed[:, :, cut] = total.astype(bf16)
                for slot, peer in enumerate(far_peers):
                    copy = remote_copy(
                        summed.at[:, rows(peer[1] // 2, share), cut],
                        got_planes.at[slot, :, :, cut],
                        send2.at[slot, chunk], recv2.at[slot, chunk], peer,
                    )
                    copy.start()
                    over_planes.append((chunk, copy))
            back, passed = [], []
            place = rows(side * pairs + p // 2, share)
            for chunk, cut in enumerate(cuts):
                for number, copy in over_planes:
                    if number == chunk:
                        copy.wait()
                total = summed[:, rows(p // 2, share), cut].astype(f32)
                for slot in range(pairs - 1):
                    total = total + got_planes[slot, :, :, cut].astype(f32)
                block[:, :, cut] = total.astype(bf16)
                for slot, peer in enumerate(far_peers):
                    copy = remote_copy(
                        block.at[:, :, cut], whole.at[:, place, cut],
                        send3.at[slot, chunk], recv3.at[slot, chunk], peer,
                    )
                    copy.start()
                    back.append((slot, chunk, copy))
                copy = remote_copy(
                    block.at[:, :, cut], whole.at[:, place, cut],
                    send9.at[pairs - 1, chunk], recv9.at[pairs - 1, chunk], sibling,
                )
                copy.start()
                passed.append(copy)
                whole[:, place, cut] = block[:, :, cut]
            for slot, chunk, copy in back:
                copy.wait()
                source = lax.rem(p + planes - 2 * (slot + 1), planes) // 2
                there = whole.at[:, rows(side * pairs + source, share), cuts[chunk]]
                relay = remote_copy(
                    there, there, send9.at[slot, chunk], recv9.at[slot, chunk], sibling
                )
                relay.start()
                passed.append(relay)
            for copy in passed:
                copy.wait()

            real, imag = newton_turned(whole[0].astype(f32), whole[1].astype(f32))
            rounded[0] = real
            rounded[1] = imag
            mine = rows(side, middle)
            first = []
            for slot, peer in enumerate(string_peers):
                copy = remote_copy(
                    rounded.at[:, mine, :], inverse.at[k, :, mine, :],
                    send4.at[slot], recv4.at[slot], peer,
                )
                copy.start()
                first.append(copy)
            inverse[k, 0] = real
            inverse[k, 1] = imag
            second = []
            for slot, copy in enumerate(first):
                copy.wait()
                source = lax.rem(k + strings - slot - 1, strings)
                relay = remote_copy(
                    inverse.at[source, :, mine, :], inverse.at[source, :, mine, :],
                    send5.at[slot], recv5.at[slot], sibling,
                )
                relay.start()
                second.append(relay)
            for relay in second:
                relay.wait()

        def find_gradient(chain_ref, wide):
            def element(index, total):
                link = lax.rem(index + strings - wide, strings)
                before = lax.rem(index + strings - wide - 1, strings)

                def product(left, right):
                    return jnp.dot(left, right, preferred_element_type=f32)

                x_re, x_im = inverse[link, 0], inverse[link, 1]
                next_re, next_im = chain_ref[index + 2, 0], chain_ref[index + 2, 1]
                a_re = product(x_re, next_re) - product(x_im, next_im)
                a_im = product(x_re, next_im) + product(x_im, next_re)
                x_re, x_im = inverse[before, 0], inverse[before, 1]
                last_re, last_im = chain_ref[index, 0], chain_ref[index, 1]
                c_re = (product(x_re, last_re) + product(x_im, last_im)).astype(bf16)
                c_im = (product(x_re, last_im) - product(x_im, last_re)).astype(bf16)
                g_re = a_im - c_im.astype(f32)
                g_im = c_re.astype(f32) - a_re
                grad[index, 0] = g_re
                grad[index, 1] = g_im
                square = g_re * g_re + g_im * g_im
                lanes = square[:, :128]
                for group in range(1, piece // 128):
                    lanes = lanes + square[:, group * 128 : (group + 1) * 128]
                sums = jnp.sum(lanes.reshape(bands // 8, 8, 128), 0)
                inside = jnp.logical_and(index >= wide, index < wide + strings)
                return total + jnp.where(inside, sums, jnp.zeros_like(sums))

            tile[...] = lax.fori_loop(
                0, strings + 2 * wide, element, jnp.zeros((8, 128), f32)
            )
            copies = [
                remote_copy(tile, first.at[k], send6.at[slot], recv6.at[slot], peer)
                for slot, peer in enumerate(string_peers)
            ]
            for copy in copies:
                copy.start()
            first[k] = tile[...]
            for copy in copies:
                copy.wait()
            stage[...] = jnp.sum(first[...], 0)
            copies = [
                remote_copy(stage, second.at[p], send7.at[slot], recv7.at[slot], peer)
                for slot, peer in enumerate(plane_peers)
            ]
            for copy in copies:
                copy.start()
            second[p] = stage[...]
            for copy in copies:
                copy.wait()
            total = jnp.sum(second[...], 0)
            total = jnp.sum(jnp.sum(total, axis=0, keepdims=True), axis=1, keepdims=True)
            return TAU_STEP / jnp.sqrt(total / count_all + EPS_NORM)

        def renewed(chain_ref, index, part_index, scale):
            old = chain_ref[index + 1, part_index].astype(f32)
            return (old + grad[index, part_index] * scale).astype(bf16)

        def renew(chain_ref, next_ref, count, scale):
            def element(index, carry):
                next_ref[index, 0] = renewed(chain_ref, index, 0, scale)
                next_ref[index, 1] = renewed(chain_ref, index, 1, scale)
                return carry

            lax.fori_loop(0, count, element, 0)

        def finish(chain_ref, next_ref, scale):
            copies = []
            mine = rows(k, piece)
            for slot, peer in enumerate(string_peers):
                for index, ref in enumerate((re_ref, im_ref)):
                    next_ref[slot, index] = renewed(chain_ref, peer[0], index, scale)
                    copy = remote_copy(
                        next_ref.at[slot, index], ref.at[:, mine],
                        send8.at[slot, index], recv8.at[slot, index], peer,
                    )
                    copy.start()
                    copies.append(copy)
            for index, ref in enumerate((re_ref, im_ref)):
                next_ref[strings - 1, index] = renewed(chain_ref, k, index, scale)
                copy = pltpu.make_async_copy(
                    next_ref.at[strings - 1, index], ref.at[:, mine], kept.at[index]
                )
                copy.start()
                copies.append(copy)
            for copy in copies:
                copy.wait()

        for turn in range(STEPS):
            wide = STEPS - 1 - turn
            find_inverses(chains[turn], wide, turn == 0)
            scale = find_gradient(chains[turn], wide)
            if wide > 0:
                renew(chains[turn], chains[turn + 1], strings + 2 * wide, scale)
        finish(chains[STEPS - 1], chains[STEPS], scale)

    vmem = pl.BlockSpec(memory_space=pltpu.VMEM)
    anywhere = pl.BlockSpec(memory_space=pl.ANY)
    square = (2, bands, bands)
    dma = pltpu.SemaphoreType.DMA
    lengths = [strings + 2 * (STEPS - step) for step in range(STEPS + 1)]
    out = jax.ShapeDtypeStruct((bands, piece * strings), bf16)
    return pl.pallas_call(
        kernel,
        out_shape=(out, out),
        in_specs=[anywhere, anywhere],
        out_specs=(vmem, vmem),
        scratch_shapes=[pltpu.VMEM((length, 2, bands, piece), bf16) for length in lengths]
        + [
            pltpu.VMEM((strings,) + square, bf16),
            pltpu.VMEM((strings - 1, 2, middle, bands), bf16),
            pltpu.VMEM((2, middle, bands), bf16),
            pltpu.VMEM((pairs - 1, 2, share, bands), bf16),
            pltpu.VMEM((2, share, bands), bf16),
            pltpu.VMEM(square, bf16),
            pltpu.VMEM(square, bf16),
            pltpu.VMEM((strings,) + square, bf16),
            pltpu.VMEM((strings, 2, middle, bands), bf16),
            pltpu.VMEM((strings, 2, middle, bands), bf16),
            pltpu.VMEM((lengths[1], 2, bands, piece), f32),
            pltpu.VMEM((8, 128), f32),
            pltpu.VMEM((strings, 8, 128), f32),
            pltpu.VMEM((8, 128), f32),
            pltpu.VMEM((planes, 8, 128), f32),
            dma((3,)),
            dma((2,)),
        ]
        + [dma((strings - 1, chunks))] * 2
        + [dma((pairs - 1, chunks))] * 4
        + [dma((strings - 1,))] * 4
        + [dma((strings - 1,))] * 2
        + [dma((planes - 1,))] * 2
        + [dma((strings - 1, 2))] * 2
        + [dma((strings,))] * 2
        + [dma((pairs, chunks))] * 2,
        compiler_params=pltpu.CompilerParams(collective_id=4, has_side_effects=True),
        name="both_steps",
    )(states, halo)


def spread_body(strings, planes, states_re, states_im, gmap):
    width = states_re.shape[2]
    total_width = width * planes
    offset = jnp.mod(gmap[0] - lax.axis_index("pw") * width, total_width)
    states, joined = spread(strings, planes, states_re[0], states_im[0])
    blocks_off, rest = offset // width, jnp.mod(offset, width)
    start = jnp.where(lax.axis_index("kstr") < STEPS, rest, width - rest)
    aligned = lax.dynamic_slice_in_dim(joined, start, width, 2)
    halo = lax.switch(
        blocks_off,
        [functools.partial(turn_blocks, strings, planes, shift) for shift in range(planes)],
        aligned,
    )
    new_re, new_im = both_steps(strings, planes, states, halo)
    return (new_re[None], new_im[None])


def solution(mesh):
    placed = (P("kstr", None, "pw"), P("kstr", None, "pw"), P("pw"))
    strings, planes = mesh.shape["kstr"], mesh.shape["pw"]

    def body(states_re, states_im, gmap):
        kpoints, bands, width = states_re.shape
        fits = (
            kpoints == 1
            and strings > 1
            and planes > 1
            and width % (strings * 128) == 0
            and bands % (planes * 16) == 0
            and bands % 128 == 0
            and planes % 2 == 0
            and planes > 2
            and strings == 2 * STEPS
        )
        if not fits:
            return general_body(states_re, states_im, gmap)
        return spread_body(strings, planes, states_re, states_im, gmap)

    return jax.shard_map(
        body,
        mesh=mesh,
        in_specs=placed,
        out_specs=(P("kstr", None, "pw"), P("kstr", None, "pw")),
        check_vma=False,
    )
```

```python
import functools

import jax
import jax.numpy as jnp
from jax import lax
from jax.experimental import pallas as pl
from jax.experimental.pallas import tpu as pltpu
from jax.sharding import PartitionSpec as P

NEWTON = 4
STEPS = 2


HIGH = lax.Precision.HIGHEST
EPS_SCALE = 1e-06
EPS_NORM = 1e-06
TAU_STEP = 0.25


def shifted(value, axis, by):
    count = lax.axis_size(axis)
    return lax.ppermute(value, axis, [(i, (i + by) % count) for i in range(count)])


def padded_2(block, sides, width):
    for axis, dim in sides:
        count = lax.axis_size(axis)
        forward = [(i, i + 1) for i in range(count - 1)]
        forward.append((count - 1, 0))
        backward = [(target, source) for source, target in forward]
        low = lax.ppermute(
            lax.slice_in_dim(block, block.shape[dim] - width, None, axis=dim), axis, forward
        )
        high = lax.ppermute(lax.slice_in_dim(block, 0, width, axis=dim), axis, backward)
        block = jnp.concatenate([low, block, high], axis=dim)
    return block


def complex_mul(left, right):

    def matmul(first, second):
        return jnp.einsum("kij,kjl->kil", first, second, precision=HIGH)

    real = matmul(left[:, 0], right[:, 0]) - matmul(left[:, 1], right[:, 1])
    imag = matmul(left[:, 0], right[:, 1]) + matmul(left[:, 1], right[:, 0])
    return jnp.stack([real, imag], 1)


def start_inverse(whole):
    magnitude = jnp.sqrt(whole[:, 0] * whole[:, 0] + whole[:, 1] * whole[:, 1])
    colmax = jnp.max(jnp.sum(magnitude, axis=1), axis=1)
    rowmax = jnp.max(jnp.sum(magnitude, axis=2), axis=1)
    factor = (1.0 / (colmax * rowmax + EPS_SCALE))[:, None, None]
    return jnp.stack(
        [jnp.swapaxes(whole[:, 0], 1, 2) * factor, -jnp.swapaxes(whole[:, 1], 1, 2) * factor], 1
    )


def newton_full(whole):
    iterate = start_inverse(whole)
    for turn in range(NEWTON):
        iterate = 2.0 * iterate - complex_mul(iterate, complex_mul(whole, iterate))
    return iterate


def bf_product(form, left, right):
    return jnp.einsum(form, left, right, preferred_element_type=jnp.float32)


def dual_terms(rounded, states):
    real = bf_product("kmn,kmg->kng", rounded[:, 0], states[:, 0]) + bf_product(
        "kmn,kmg->kng", rounded[:, 1], states[:, 1]
    )
    imag = bf_product("kmn,kmg->kng", rounded[:, 0], states[:, 1]) - bf_product(
        "kmn,kmg->kng", rounded[:, 1], states[:, 0]
    )
    return jnp.stack([real, imag], 1).astype(jnp.bfloat16)


def rotate_columns(block, amount, width):
    blocks_off = amount // width
    rest = amount % width
    plane_size = lax.axis_size("pw")
    for bit in range((plane_size - 1).bit_length()):
        moved = shifted(block, "pw", -(1 << bit))
        block = jnp.where(jnp.bitwise_and(jnp.right_shift(blocks_off, bit), 1) == 1, moved, block)
    after = shifted(block, "pw", -1)
    joined = jnp.concatenate([block, after], block.ndim - 1)
    return lax.dynamic_slice_in_dim(joined, rest, width, block.ndim - 1)


def general_body(states_re, states_im, gmap):
    kpoints, bands, width = states_re.shape
    string_size = lax.axis_size("kstr")
    plane_size = lax.axis_size("pw")
    string_index = lax.axis_index("kstr")
    total_width = width * plane_size
    offset = jnp.mod(gmap[0] - lax.axis_index("pw") * width, total_width)
    back_offset = jnp.mod(total_width - offset, total_width)
    at_first = string_index == 0
    at_last = string_index == string_size - 1
    count_all = 2 * kpoints * string_size * bands * width * plane_size
    states = jnp.stack([states_re, states_im], 1)
    for step in range(STEPS):
        padded = padded_2(states, (("kstr", 0),), 1)
        ahead = padded[-1:]
        behind = padded[:1]
        turned = rotate_columns(ahead, offset, width)
        ahead = jnp.where(at_last, turned, ahead)
        following = jnp.concatenate([states[1:], ahead], 0)
        s_re = bf_product("kmg,kng->kmn", states[:, 0], following[:, 0]) + bf_product(
            "kmg,kng->kmn", states[:, 1], following[:, 1]
        )
        s_im = bf_product("kmg,kng->kmn", states[:, 0], following[:, 1]) - bf_product(
            "kmg,kng->kmn", states[:, 1], following[:, 0]
        )
        partial_value = jnp.stack([s_re, s_im], 1)
        whole = lax.psum(partial_value, "pw") / (width * plane_size)
        inverse = newton_full(whole)
        rounded = inverse.astype(jnp.bfloat16)
        a_re = bf_product("kmn,kmg->kng", rounded[:, 0], following[:, 0]) - bf_product(
            "kmn,kmg->kng", rounded[:, 1], following[:, 1]
        )
        a_im = bf_product("kmn,kmg->kng", rounded[:, 0], following[:, 1]) + bf_product(
            "kmn,kmg->kng", rounded[:, 1], following[:, 0]
        )
        earlier = dual_terms(rounded[:-1], states[:-1])
        previous_inverse = shifted(rounded, "kstr", 1)
        arrived = dual_terms(previous_inverse, behind)
        placed = rotate_columns(arrived, back_offset, width)
        arrived = jnp.where(at_first, placed, arrived)
        incoming = jnp.concatenate([arrived, earlier], 0).astype(jnp.float32)
        g_re = a_im - incoming[:, 1]
        g_im = incoming[:, 0] - a_re
        total = lax.psum(jnp.sum(g_re * g_re + g_im * g_im), ("kstr", "pw"))
        rms = jnp.sqrt(total / count_all + EPS_NORM)
        new_re = (states[:, 0].astype(jnp.float32) + TAU_STEP * g_re / rms).astype(jnp.bfloat16)
        new_im = (states[:, 1].astype(jnp.float32) + TAU_STEP * g_im / rms).astype(jnp.bfloat16)
        states = jnp.stack([new_re, new_im], 1)
    return (states[:, 0], states[:, 1])


def halves(value):
    high = value.astype(jnp.bfloat16)
    return high, (value - high.astype(jnp.float32)).astype(jnp.bfloat16)


def left_factor(real, imag):
    real_high, real_low = halves(real)
    imag_high, imag_low = halves(imag)
    high = jnp.concatenate([real_high, imag_high], 1)
    return jnp.concatenate([high, high, real_low, imag_low], 1)


def right_factor(real, imag):
    real_high, real_low = halves(real)
    imag_high, imag_low = halves(imag)
    high = [
        jnp.concatenate([real_high, imag_high], 1),
        jnp.concatenate([-imag_high, real_high], 1),
    ]
    low = [
        jnp.concatenate([real_low, imag_low], 1),
        jnp.concatenate([-imag_low, real_low], 1),
    ]
    return jnp.concatenate(high + low + high, 0)


def newton_turned(real, imag):
    bands = real.shape[0]
    magnitude = jnp.sqrt(real * real + imag * imag)
    colmax = jnp.max(jnp.sum(magnitude, axis=0, keepdims=True), axis=1, keepdims=True)
    rowmax = jnp.max(jnp.sum(magnitude, axis=1, keepdims=True), axis=0, keepdims=True)
    factor = 1.0 / (colmax * rowmax + EPS_SCALE)
    x_re, x_im = real.T * factor, -imag.T * factor
    whole = left_factor(real, imag)
    for turn in range(NEWTON):
        p = jnp.dot(whole, right_factor(x_re, x_im), preferred_element_type=jnp.float32)
        q = jnp.dot(
            left_factor(x_re, x_im),
            right_factor(p[:, :bands], p[:, bands:]),
            preferred_element_type=jnp.float32,
        )
        x_re = 2.0 * x_re - q[:, :bands]
        x_im = 2.0 * x_im - q[:, bands:]
    return x_re.T.astype(jnp.bfloat16), x_im.T.astype(jnp.bfloat16)


def remote_copy(source, place, send, recv, target):
    return pltpu.make_async_remote_copy(
        src_ref=source,
        dst_ref=place,
        send_sem=send,
        recv_sem=recv,
        device_id=target,
        device_id_type=pl.DeviceIdType.MESH,
    )


def greet_all(greeted, awaited):
    barrier = pltpu.get_barrier_semaphore()
    for peer in greeted:
        pl.semaphore_signal(barrier, inc=1, device_id=peer, device_id_type=pl.DeviceIdType.MESH)
    pl.semaphore_wait(barrier, awaited)


def spread(strings, planes, states_re, states_im):
    bands, width = states_re.shape
    piece = width // strings

    def kernel(re_ref, im_ref, out_ref, joined_ref, send, recv, local):
        k, p = lax.axis_index("kstr"), lax.axis_index("pw")
        forward = (k < STEPS).astype(jnp.int32)
        giver = (k, lax.rem(p + planes - 1 + 2 * forward, planes))
        taker = (k, lax.rem(p + planes + 1 - 2 * forward, planes))
        string_peers = [(lax.rem(k + step, strings), p) for step in range(1, strings)]
        greet_all(string_peers + [giver], strings)
        kept = pl.ds(pl.multiple_of((1 - forward) * width, width), width)
        other = pl.ds(pl.multiple_of(forward * width, width), width)
        mine = pl.ds(pl.multiple_of(k * piece, piece), piece)
        copies, inside = [], []
        for part, ref in enumerate((re_ref, im_ref)):
            for slot, peer in enumerate(string_peers):
                cut = pl.ds(pl.multiple_of(peer[0] * piece, piece), piece)
                copies.append(
                    remote_copy(
                        ref.at[:, cut], out_ref.at[k, part], send.at[slot, part], recv.at[slot, part], peer
                    )
                )
            slot = strings - 1
            copies.append(
                remote_copy(
                    ref, joined_ref.at[part, :, other], send.at[slot, part], recv.at[slot, part], taker
                )
            )
            inside.append(
                pltpu.make_async_copy(ref, joined_ref.at[part, :, kept], local.at[0, part])
            )
            inside.append(
                pltpu.make_async_copy(ref.at[:, mine], out_ref.at[k, part], local.at[1, part])
            )
        for copy in copies + inside:
            copy.start()
        for copy in inside + copies:
            copy.wait()

    vmem = pl.BlockSpec(memory_space=pltpu.VMEM)
    return pl.pallas_call(
        kernel,
        out_shape=(
            jax.ShapeDtypeStruct((strings, 2, bands, piece), states_re.dtype),
            jax.ShapeDtypeStruct((2, bands, 2 * width), states_re.dtype),
        ),
        in_specs=[vmem, vmem],
        out_specs=(vmem, vmem),
        scratch_shapes=[
            pltpu.SemaphoreType.DMA((strings, 2)),
            pltpu.SemaphoreType.DMA((strings, 2)),
            pltpu.SemaphoreType.DMA((2, 2)),
        ],
        compiler_params=pltpu.CompilerParams(collective_id=1, has_side_effects=True),
        name="spread",
    )(states_re, states_im)


def turn_blocks(strings, planes, shift, aligned):
    _, bands, width = aligned.shape
    piece = width // strings

    def kernel(block_ref, out_ref, send, recv, local):
        k, p = lax.axis_index("kstr"), lax.axis_index("pw")
        up, down = lax.rem(p + shift, planes), lax.rem(p + planes - shift, planes)
        steps = range(1 if shift == 0 else 0, strings)
        forward = (k < STEPS).astype(jnp.int32)
        target_plane = forward * down + (1 - forward) * up
        givers, takers = [], []
        for step in steps:
            other = lax.rem(k + strings - step, strings)
            ahead = (other < STEPS).astype(jnp.int32)
            givers.append((other, ahead * up + (1 - ahead) * down))
            takers.append((lax.rem(k + step, strings), target_plane))
        greet_all(givers, len(takers))
        copies = []
        for slot, taker in enumerate(takers):
            cut = pl.ds(pl.multiple_of(taker[0] * piece, piece), piece)
            copies.append(
                remote_copy(
                    block_ref.at[:, :, cut], out_ref.at[k], send.at[slot], recv.at[slot], taker
                )
            )
        for copy in copies:
            copy.start()
        if shift == 0:
            cut = pl.ds(pl.multiple_of(k * piece, piece), piece)
            inside = pltpu.make_async_copy(block_ref.at[:, :, cut], out_ref.at[k], local.at[0])
            inside.start()
            inside.wait()
        for copy in copies:
            copy.wait()

    vmem = pl.BlockSpec(memory_space=pltpu.VMEM)
    return pl.pallas_call(
        kernel,
        out_shape=jax.ShapeDtypeStruct((strings, 2, bands, piece), aligned.dtype),
        in_specs=[vmem],
        out_specs=vmem,
        scratch_shapes=[
            pltpu.SemaphoreType.DMA((strings,)),
            pltpu.SemaphoreType.DMA((strings,)),
            pltpu.SemaphoreType.DMA((1,)),
        ],
        compiler_params=pltpu.CompilerParams(collective_id=20 + shift, has_side_effects=True),
        name=f"turn_{shift}",
    )(aligned)


def margin_of(own, ahead):
    left = jnp.concatenate([own[0], own[1]], 1)
    form = (((1,), (1,)), ((), ()))
    real = lax.dot_general(
        left, jnp.concatenate([ahead[0], ahead[1]], 1), form, preferred_element_type=jnp.float32
    )
    imag = lax.dot_general(
        left, jnp.concatenate([ahead[1], -ahead[0]], 1), form, preferred_element_type=jnp.float32
    )
    return real, imag


def both_steps(strings, planes, states, halo):
    _, _, bands, piece = states.shape
    total_width = piece * strings * planes
    count_all = 2 * strings * bands * total_width
    share, middle, pairs = bands // planes, bands // 2, planes // 2
    chunks = bands // 128
    bf16, f32 = jnp.bfloat16, jnp.float32

    def kernel(states_ref, halo_ref, re_ref, im_ref, *scratch):
        chains, scratch = scratch[: STEPS + 1], scratch[STEPS + 1 :]
        part, got_string, summed, got_planes, block, whole, rounded, inverse = scratch[:8]
        got_pair, half, scratch = scratch[8], scratch[9], scratch[:8] + scratch[10:]
        grad, tile, first, stage, second, load, kept = scratch[8:15]
        send1, recv1, send2, recv2, send3, recv3, send4, recv4, send5, recv5 = scratch[15:25]
        send6, recv6, send7, recv7, send8, recv8 = scratch[25:31]
        send0, recv0, send9, recv9 = scratch[31:]
        k, p = lax.axis_index("kstr"), lax.axis_index("pw")
        string_peers = [(lax.rem(k + step, strings), p) for step in range(1, strings)]
        plane_peers = [(k, lax.rem(p + step, planes)) for step in range(1, planes)]
        far_peers = [(k, lax.rem(p + 2 * step, planes)) for step in range(1, pairs)]
        side = lax.rem(p, 2)
        sibling = (k, p + 1 - 2 * side)

        def rows(index, size):
            return pl.ds(pl.multiple_of(index * size, size), size)

        barrier = pltpu.get_barrier_semaphore()
        for peer in string_peers + plane_peers:
            pl.semaphore_signal(
                barrier, inc=1, device_id=peer, device_id_type=pl.DeviceIdType.MESH
            )

        loads = [
            pltpu.make_async_copy(
                halo_ref.at[strings - STEPS :], chains[0].at[:STEPS], load.at[0]
            ),
            pltpu.make_async_copy(states_ref, chains[0].at[STEPS : STEPS + strings], load.at[1]),
            pltpu.make_async_copy(
                halo_ref.at[:STEPS], chains[0].at[STEPS + strings :], load.at[2]
            ),
        ]
        for copy in loads:
            copy.start()
        for copy in loads:
            copy.wait()
        cuts = [pl.ds(chunk * 128, 128) for chunk in range(chunks)]

        def put_margin(chain_ref, wide, slot, which):
            real, imag = margin_of(chain_ref[wide + 1 + which], chain_ref[wide + 2 + which])
            part[slot, 0] = (real * (1.0 / total_width)).astype(bf16)
            part[slot, 1] = (imag * (1.0 / total_width)).astype(bf16)

        def find_inverses(chain_ref, wide, opening):
            pair, over_string = [], []

            def carry_on(slot):
                pair[slot].wait()
                both = part[slot, :, rows(side, middle), :].astype(f32)
                half[slot] = (both + got_pair[slot].astype(f32)).astype(bf16)
                if slot == strings - 1:
                    return
                for chunk, cut in enumerate(cuts):
                    copy = remote_copy(
                        half.at[slot, :, :, cut], got_string.at[slot, :, :, cut],
                        send1.at[slot, chunk], recv1.at[slot, chunk], string_peers[slot],
                    )
                    copy.start()
                    over_string.append((chunk, copy))

            for slot in range(strings):
                which = k if slot == strings - 1 else string_peers[slot][0]
                put_margin(chain_ref, wide, slot, which)
                if opening and slot == 0:
                    pl.semaphore_wait(barrier, len(string_peers) + len(plane_peers))
                copy = remote_copy(
                    part.at[slot, :, rows(1 - side, middle), :], got_pair.at[slot],
                    send0.at[slot], recv0.at[slot], sibling,
                )
                copy.start()
                pair.append(copy)
                if slot > 0:
                    carry_on(slot - 1)
            carry_on(strings - 1)

            over_planes = []
            for chunk, cut in enumerate(cuts):
                for number, copy in over_string:
                    if number == chunk:
                        copy.wait()
                total = half[strings - 1, :, :, cut].astype(f32)
                for slot in range(strings - 1):
                    total = total + got_string[slot, :, :, cut].astype(f32)
                summed[:, :, cut] = total.astype(bf16)
                for slot, peer in enumerate(far_peers):
                    copy = remote_copy(
                        summed.at[:, rows(peer[1] // 2, share), cut],
                        got_planes.at[slot, :, :, cut],
                        send2.at[slot, chunk], recv2.at[slot, chunk], peer,
                    )
                    copy.start()
                    over_planes.append((chunk, copy))
            back, passed = [], []
            place = rows(side * pairs + p // 2, share)
            for chunk, cut in enumerate(cuts):
                for number, copy in over_planes:
                    if number == chunk:
                        copy.wait()
                total = summed[:, rows(p // 2, share), cut].astype(f32)
                for slot in range(pairs - 1):
                    total = total + got_planes[slot, :, :, cut].astype(f32)
                block[:, :, cut] = total.astype(bf16)
                for slot, peer in enumerate(far_peers):
                    copy = remote_copy(
                        block.at[:, :, cut], whole.at[:, place, cut],
                        send3.at[slot, chunk], recv3.at[slot, chunk], peer,
                    )
                    copy.start()
                    back.append((slot, chunk, copy))
                copy = remote_copy(
                    block.at[:, :, cut], whole.at[:, place, cut],
                    send9.at[pairs - 1, chunk], recv9.at[pairs - 1, chunk], sibling,
                )
                copy.start()
                passed.append(copy)
                whole[:, place, cut] = block[:, :, cut]
            for slot, chunk, copy in back:
                copy.wait()
                source = lax.rem(p + planes - 2 * (slot + 1), planes) // 2
                there = whole.at[:, rows(side * pairs + source, share), cuts[chunk]]
                relay = remote_copy(
                    there, there, send9.at[slot, chunk], recv9.at[slot, chunk], sibling
                )
                relay.start()
                passed.append(relay)
            for copy in passed:
                copy.wait()

            real, imag = newton_turned(whole[0].astype(f32), whole[1].astype(f32))
            rounded[0] = real
            rounded[1] = imag
            mine = rows(side, middle)
            first = []
            for slot, peer in enumerate(string_peers):
                copy = remote_copy(
                    rounded.at[:, mine, :], inverse.at[k, :, mine, :],
                    send4.at[slot], recv4.at[slot], peer,
                )
                copy.start()
                first.append(copy)
            inverse[k, 0] = real
            inverse[k, 1] = imag
            second = []
            for slot, copy in enumerate(first):
                copy.wait()
                source = lax.rem(k + strings - slot - 1, strings)
                relay = remote_copy(
                    inverse.at[source, :, mine, :], inverse.at[source, :, mine, :],
                    send5.at[slot], recv5.at[slot], sibling,
                )
                relay.start()
                second.append(relay)
            for relay in second:
                relay.wait()

        def find_gradient(chain_ref, wide):
            def element(index, total):
                link = lax.rem(index + strings - wide, strings)
                before = lax.rem(index + strings - wide - 1, strings)

                def product(left, right):
                    return jnp.dot(left, right, preferred_element_type=f32)

                x_re, x_im = inverse[link, 0], inverse[link, 1]
                next_re, next_im = chain_ref[index + 2, 0], chain_ref[index + 2, 1]
                a_re = product(x_re, next_re) - product(x_im, next_im)
                a_im = product(x_re, next_im) + product(x_im, next_re)
                x_re, x_im = inverse[before, 0], inverse[before, 1]
                last_re, last_im = chain_ref[index, 0], chain_ref[index, 1]
                c_re = (product(x_re, last_re) + product(x_im, last_im)).astype(bf16)
                c_im = (product(x_re, last_im) - product(x_im, last_re)).astype(bf16)
                g_re = a_im - c_im.astype(f32)
                g_im = c_re.astype(f32) - a_re
                grad[index, 0] = g_re
                grad[index, 1] = g_im
                square = g_re * g_re + g_im * g_im
                lanes = square[:, :128]
                for group in range(1, piece // 128):
                    lanes = lanes + square[:, group * 128 : (group + 1) * 128]
                sums = jnp.sum(lanes.reshape(bands // 8, 8, 128), 0)
                return total + sums

            nothing = jnp.zeros((8, 128), f32)
            tile[...] = lax.fori_loop(wide, wide + strings, element, nothing)
            copies = [
                remote_copy(tile, first.at[k], send6.at[slot], recv6.at[slot], peer)
                for slot, peer in enumerate(string_peers)
            ]
            for copy in copies:
                copy.start()
            first[k] = tile[...]
            for edge in range(wide):
                element(edge, nothing)
                element(wide + strings + edge, nothing)
            for copy in copies:
                copy.wait()
            stage[...] = jnp.sum(first[...], 0)
            copies = [
                remote_copy(stage, second.at[p], send7.at[slot], recv7.at[slot], peer)
                for slot, peer in enumerate(plane_peers)
            ]
            for copy in copies:
                copy.start()
            second[p] = stage[...]
            for copy in copies:
                copy.wait()
            total = jnp.sum(second[...], 0)
            total = jnp.sum(jnp.sum(total, axis=0, keepdims=True), axis=1, keepdims=True)
            return TAU_STEP / jnp.sqrt(total / count_all + EPS_NORM)

        def renewed(chain_ref, index, part_index, scale):
            old = chain_ref[index + 1, part_index].astype(f32)
            return (old + grad[index, part_index] * scale).astype(bf16)

        def renew(chain_ref, next_ref, count, scale):
            def element(index, carry):
                next_ref[index, 0] = renewed(chain_ref, index, 0, scale)
                next_ref[index, 1] = renewed(chain_ref, index, 1, scale)
                return carry

            lax.fori_loop(0, count, element, 0)

        def finish(chain_ref, next_ref, scale):
            copies = []
            mine = rows(k, piece)
            for slot, peer in enumerate(string_peers):
                for index, ref in enumerate((re_ref, im_ref)):
                    next_ref[slot, index] = renewed(chain_ref, peer[0], index, scale)
                    copy = remote_copy(
                        next_ref.at[slot, index], ref.at[:, mine],
                        send8.at[slot, index], recv8.at[slot, index], peer,
                    )
                    copy.start()
                    copies.append(copy)
            for index, ref in enumerate((re_ref, im_ref)):
                next_ref[strings - 1, index] = renewed(chain_ref, k, index, scale)
                copy = pltpu.make_async_copy(
                    next_ref.at[strings - 1, index], ref.at[:, mine], kept.at[index]
                )
                copy.start()
                copies.append(copy)
            for copy in copies:
                copy.wait()

        for turn in range(STEPS):
            wide = STEPS - 1 - turn
            find_inverses(chains[turn], wide, turn == 0)
            scale = find_gradient(chains[turn], wide)
            if wide > 0:
                renew(chains[turn], chains[turn + 1], strings + 2 * wide, scale)
        finish(chains[STEPS - 1], chains[STEPS], scale)

    vmem = pl.BlockSpec(memory_space=pltpu.VMEM)
    anywhere = pl.BlockSpec(memory_space=pl.ANY)
    square = (2, bands, bands)
    dma = pltpu.SemaphoreType.DMA
    lengths = [strings + 2 * (STEPS - step) for step in range(STEPS + 1)]
    out = jax.ShapeDtypeStruct((bands, piece * strings), bf16)
    return pl.pallas_call(
        kernel,
        out_shape=(out, out),
        in_specs=[anywhere, anywhere],
        out_specs=(vmem, vmem),
        scratch_shapes=[pltpu.VMEM((length, 2, bands, piece), bf16) for length in lengths]
        + [
            pltpu.VMEM((strings,) + square, bf16),
            pltpu.VMEM((strings - 1, 2, middle, bands), bf16),
            pltpu.VMEM((2, middle, bands), bf16),
            pltpu.VMEM((pairs - 1, 2, share, bands), bf16),
            pltpu.VMEM((2, share, bands), bf16),
            pltpu.VMEM(square, bf16),
            pltpu.VMEM(square, bf16),
            pltpu.VMEM((strings,) + square, bf16),
            pltpu.VMEM((strings, 2, middle, bands), bf16),
            pltpu.VMEM((strings, 2, middle, bands), bf16),
            pltpu.VMEM((lengths[1], 2, bands, piece), f32),
            pltpu.VMEM((8, 128), f32),
            pltpu.VMEM((strings, 8, 128), f32),
            pltpu.VMEM((8, 128), f32),
            pltpu.VMEM((planes, 8, 128), f32),
            dma((3,)),
            dma((2,)),
        ]
        + [dma((strings - 1, chunks))] * 2
        + [dma((pairs - 1, chunks))] * 4
        + [dma((strings - 1,))] * 4
        + [dma((strings - 1,))] * 2
        + [dma((planes - 1,))] * 2
        + [dma((strings - 1, 2))] * 2
        + [dma((strings,))] * 2
        + [dma((pairs, chunks))] * 2,
        compiler_params=pltpu.CompilerParams(collective_id=4, has_side_effects=True),
        name="both_steps",
    )(states, halo)


def spread_body(strings, planes, states_re, states_im, gmap):
    width = states_re.shape[2]
    total_width = width * planes
    offset = jnp.mod(gmap[0] - lax.axis_index("pw") * width, total_width)
    states, joined = spread(strings, planes, states_re[0], states_im[0])
    blocks_off, rest = offset // width, jnp.mod(offset, width)
    start = jnp.where(lax.axis_index("kstr") < STEPS, rest, width - rest)
    aligned = lax.dynamic_slice_in_dim(joined, start, width, 2)
    halo = lax.switch(
        blocks_off,
        [functools.partial(turn_blocks, strings, planes, shift) for shift in range(planes)],
        aligned,
    )
    new_re, new_im = both_steps(strings, planes, states, halo)
    return (new_re[None], new_im[None])


def solution(mesh):
    placed = (P("kstr", None, "pw"), P("kstr", None, "pw"), P("pw"))
    strings, planes = mesh.shape["kstr"], mesh.shape["pw"]

    def body(states_re, states_im, gmap):
        kpoints, bands, width = states_re.shape
        fits = (
            kpoints == 1
            and strings > 1
            and planes > 1
            and width % (strings * 128) == 0
            and bands % (planes * 16) == 0
            and bands % 128 == 0
            and planes % 2 == 0
            and planes > 2
            and strings == 2 * STEPS
        )
        if not fits:
            return general_body(states_re, states_im, gmap)
        return spread_body(strings, planes, states_re, states_im, gmap)

    return jax.shard_map(
        body,
        mesh=mesh,
        in_specs=placed,
        out_specs=(P("kstr", None, "pw"), P("kstr", None, "pw")),
        check_vma=False,
    )
```
